256 devices in a mesh: bricks: 4 (over x), grp: 64 (over z, y, core).
Axes of the slice: x: 4, y: 4, z: 8, core: 2. Of those that a mesh axis runs over, the one named last changes fastest.
Arguments:
- features: bfloat16 [2048, 64, 512], P(('bricks', 'grp')), may hold values from -6 to 6
- occupancy: int32 [2048, 512], P(('bricks', 'grp')), may hold values from 0 to 1
- neighbours: int32 [2048, 26], P(('bricks', 'grp')), may hold values from -1 to 2047, as said below
- coarse_map: int32 [2048], P(('bricks', 'grp')), may hold values from 0 to 2047, as said below
- norm_gain: float32 [64], replicated, may hold values from 0.1 to 1.9
- time_shift: float32 [64], replicated, may hold values from -4 to 4
- conv_weight: bfloat16 [27, 64, 64], replicated, may hold values from -0.15625 to 0.15625
- stride_weight: bfloat16 [8, 64, 128], replicated, may hold values from -0.25 to 0.25
- coarse_bias: float32 [128], replicated, may hold values from -3 to 3
Outputs:
- fine_out: bfloat16 [2048, 64, 512], P(('bricks', 'grp'))
- coarse_out: bfloat16 [256, 128, 512], P(('bricks', 'grp'))
The draws below stay inside these ranges and needn't reach their ends.
Inputs may be any that keep to these rules, and one draw needn't show every extreme that they name: The key orders bricks by x-slab: brick i lies on device i // 8 of bricks+grp, in the slab of cells with x coordinate i // 8. neighbours[i, o] names the brick at offset o from brick i, or -1 where that cell holds no active brick or lies outside the grid. `coarse_map`: every coarse brick has all eight octants, each named once. Coarse brick c is held by device c // 1. Its eight children lie four on device 2 k and four on device 2 k + 1, with k = c // 2; so each device holds the coarse bricks of exactly 4 of its own bricks, and the coarse bricks of its other 4 bricks are held by the device whose index differs in the lowest bit.
All inputs are finite; a program needn't handle non-finite values.
Results may differ from the reference program's by a relative error of at most 0.0047.
Values may be sent and summed in bfloat16 or wider, within the bound.
No kernel may reach another device: no remote copies, remote signals or barrier semaphores. Data moves between devices by JAX's collectives and lax.ppermute only.
A program may use at most 128 MiB of HBM per device.

```python
import jax
import jax.numpy as jnp
from jax import lax

C = 64
C2 = 128
VOX = 512
BRK_DEV = 8
NSLAB = 256
NBRICK = 2048


def layout(key):
    quads = BRK_DEV // 2
    pairs = NSLAB // 2
    pair_keys = jax.random.split(jax.random.fold_in(key, 7), pairs)
    chosen = jax.vmap(lambda single: jax.random.permutation(single, quads))(pair_keys)[:, :BRK_DEV // 4]
    quad_on = jnp.zeros((pairs, quads), jnp.int32).at[jnp.arange(pairs)[:, None], chosen].set(1)
    cell_y = jnp.arange(2 * BRK_DEV) // 8
    cell_z = jnp.arange(2 * BRK_DEV) % 8
    cell_quad = cell_y // 2 * 4 + cell_z // 2
    cell_on = jnp.repeat(quad_on[:, cell_quad], 2, axis=0)
    cell_rank = jnp.cumsum(cell_on, axis=1) - 1
    cell_of = jax.vmap(lambda row: jnp.nonzero(row, size=BRK_DEV)[0])(cell_on).astype(jnp.int32)
    return (cell_on, cell_rank, cell_of, quad_on)


def draw_neighbours(key, part):
    cell_on, cell_rank, cell_of, quad_on = layout(key)
    slab = jnp.arange(NSLAB, dtype=jnp.int32)[:, None]
    pos_y = cell_of // 8
    pos_z = cell_of % 8
    extent_y = BRK_DEV // 4
    columns = []
    for shift_x in (-1, 0, 1):
        for shift_y in (-1, 0, 1):
            for shift_z in (-1, 0, 1):
                if shift_x == 0 and shift_y == 0 and (shift_z == 0):
                    continue
                target_x = slab + shift_x + 0 * pos_y
                target_y = pos_y + shift_y
                target_z = pos_z + shift_z
                inside = (target_x >= 0) & (target_x < NSLAB) & (target_y >= 0) & (target_y < extent_y) & (target_z >= 0) & (target_z < 8)
                clip_x = jnp.clip(target_x, 0, NSLAB - 1)
                clip_cell = jnp.clip(target_y, 0, extent_y - 1) * 8 + jnp.clip(target_z, 0, 7)
                present = cell_on[clip_x, clip_cell] == 1
                target = clip_x * BRK_DEV + cell_rank[clip_x, clip_cell]
                columns.append(jnp.where(inside & present, target, -1))
    return jnp.stack(columns, axis=-1).reshape(NSLAB * BRK_DEV, 26).astype(jnp.int32)


def draw_coarse_map(key, part):
    cell_on, cell_rank, cell_of, quad_on = layout(key)
    pairs = NSLAB // 2
    quad_rank = jnp.cumsum(quad_on, axis=1) - 1
    perm_keys = jax.random.split(jax.random.fold_in(key, 11), pairs)
    relabel = jax.vmap(lambda single: jax.random.permutation(single, BRK_DEV // 4))(perm_keys).astype(jnp.int32)
    slab = jnp.arange(NSLAB, dtype=jnp.int32)[:, None] + 0 * cell_of
    pos_y = cell_of // 8
    pos_z = cell_of % 8
    quad = pos_y // 2 * 4 + pos_z // 2
    ranked = quad_rank[slab // 2, quad]
    shuffled = relabel[slab // 2, ranked]
    coarse_id = slab // 2 * (BRK_DEV // 4) + shuffled
    octant = slab % 2 * 4 + pos_y % 2 * 2 + pos_z % 2
    return (coarse_id * 8 + octant).reshape(-1).astype(jnp.int32)


def draw_occupancy(key, part):
    total = NSLAB * BRK_DEV
    density = jax.random.randint(jax.random.fold_in(key, 3), (total, 1), 250, 900)
    rolled = jax.random.randint(jax.random.fold_in(key, 5), (total, VOX), 0, 1000)
    return (rolled < density).astype(jnp.int32)


def level_of(stream_key, dims, cuts, low, largest):
    factor_of = 1.0
    for axis_at, parts in cuts:
        heights = jax.random.uniform(jax.random.fold_in(jax.random.fold_in(stream_key, 6), axis_at), (parts,), jnp.float32, low / len(cuts), largest / len(cuts))
        factor_of = factor_of * jnp.repeat(jnp.exp(heights), dims[axis_at] // parts).reshape((-1,) + (1,) * (len(dims) - 1 - axis_at))
    return factor_of


def normal_values(own_key, shape, scale, bound, cuts=(), held_as=jnp.bfloat16):
    entries = scale * jax.random.normal(own_key, shape, jnp.float32)
    if cuts:
        entries = entries * level_of(own_key, shape, cuts, -0.22, 0.18)
    return jnp.clip(entries, -bound, bound).astype(held_as)


def setup_inputs(seed: int = 0) -> dict:
    splits = jax.random.split(jax.random.key(seed), 10)
    return {
        "features": normal_values(splits[0], (NBRICK, C, VOX), 1.0, 6.0, ((0, 256),)),
        "occupancy": draw_occupancy(jax.random.fold_in(splits[9], 71), 0),
        "neighbours": draw_neighbours(jax.random.fold_in(splits[9], 71), 0),
        "coarse_map": draw_coarse_map(jax.random.fold_in(splits[9], 71), 0),
        "norm_gain": jnp.clip(1.0 + 0.18 * jax.random.normal(splits[4], (C,), jnp.float32), 0.1, 1.9),
        "time_shift": normal_values(splits[5], (C,), 1.0, 4.0, (), jnp.float32),
        "conv_weight": normal_values(splits[6], (27, C, C), (27 * C) ** -0.5, 0.15625),
        "stride_weight": normal_values(splits[7], (8, C, C2), (8 * C) ** -0.5, 0.25),
        "coarse_bias": normal_values(splits[8], (C2,), 0.5, 3.0, (), jnp.float32),
    }


norm_eps = 1e-06

def activate(features, occupancy, norm_gain):
    values = features.astype(jnp.float32)
    scale = lax.rsqrt(lax.optimization_barrier(jnp.mean(values * values, axis=1, keepdims=True)) + norm_eps)
    normed = values * scale * norm_gain[None, :, None]
    mask = occupancy[:, None, :].astype(jnp.float32)
    return (jax.nn.silu(normed) * mask).astype(jnp.bfloat16)

def layer_slice(cubes, axis_pos, shift):
    if shift == -1:
        return lax.slice_in_dim(cubes, 7, 8, axis=axis_pos)
    if shift == 1:
        return lax.slice_in_dim(cubes, 0, 1, axis=axis_pos)
    return cubes

def assemble(center, fetch):
    bricks_here = center.shape[0]
    channels = center.shape[1]
    cube = center.reshape(bricks_here, channels, 8, 8, 8)
    planes = []
    position = 0
    for shift_x in (-1, 0, 1):
        rows_y = []
        for shift_y in (-1, 0, 1):
            cols_z = []
            for shift_z in (-1, 0, 1):
                if shift_x == 0 and shift_y == 0 and (shift_z == 0):
                    cols_z.append(cube)
                else:
                    cols_z.append(fetch(position, shift_x, shift_y, shift_z))
                    position += 1
            rows_y.append(jnp.concatenate(cols_z, axis=4))
        planes.append(jnp.concatenate(rows_y, axis=3))
    return jnp.concatenate(planes, axis=2)

def convolve(padded, conv_weight):
    bricks_here = padded.shape[0]
    channels = padded.shape[1]
    total = jnp.zeros((bricks_here, conv_weight.shape[2], 512), jnp.float32)
    for start_x in range(3):
        for start_y in range(3):
            taps = []
            for start_z in range(3):
                window = padded[:, :, start_x:start_x + 8, start_y:start_y + 8, start_z:start_z + 8]
                taps.append(window.reshape(bricks_here, channels, 512))
            stacked = jnp.concatenate(taps, axis=1).astype(jnp.float32)
            first_tap = 9 * start_x + 3 * start_y
            weight = conv_weight[first_tap:first_tap + 3].reshape(3 * channels, -1).astype(jnp.float32)
            total = total + jnp.einsum('bcp,cd->bdp', stacked, weight)
    return total

def reduce_resolution(fine_features, stride_weight, coarse_bias):
    bricks_here = fine_features.shape[0]
    channels = fine_features.shape[1]
    split = fine_features.reshape(bricks_here, channels, 4, 2, 4, 2, 4, 2).astype(jnp.float32)
    kernel = stride_weight.reshape(2, 2, 2, channels, -1).astype(jnp.float32)
    octant = jnp.einsum('nciajbkd,abdce->neijk', split, kernel)
    octant = octant + coarse_bias[None, :, None, None, None]
    return octant.reshape(bricks_here, -1).astype(jnp.bfloat16)

def assemble_coarse(placed, coarse_count):
    wide = placed.shape[1] // 64
    shaped = placed.reshape(coarse_count, 2, 2, 2, wide, 4, 4, 4)
    return shaped.transpose(0, 4, 1, 5, 2, 6, 3, 7).reshape(coarse_count, wide, 512)

def reference(features, occupancy, neighbours, coarse_map, norm_gain, time_shift, conv_weight, stride_weight, coarse_bias):
    total_bricks = features.shape[0]
    channels = features.shape[1]
    active = activate(features, occupancy, norm_gain)
    cubes = active.reshape(total_bricks, channels, 8, 8, 8)
    block = 256 if total_bricks % 256 == 0 else total_bricks

    def one_block(number):
        start = (number * block).astype(jnp.int32)
        centre = lax.dynamic_slice_in_dim(active, start, block, 0)
        listed = lax.dynamic_slice_in_dim(neighbours, start, block, 0)
        raw = lax.dynamic_slice_in_dim(features, start, block, 0)
        mask = lax.dynamic_slice_in_dim(occupancy, start, block, 0)

        def fetch(position, shift_x, shift_y, shift_z):
            target = listed[:, position]
            rows = jnp.take(cubes, jnp.maximum(target, 0).astype(jnp.int32), axis=0)
            piece = layer_slice(layer_slice(layer_slice(rows, 2, shift_x), 3, shift_y), 4, shift_z)
            keep = (target >= 0).astype(piece.dtype)
            return piece * keep[:, None, None, None, None]
        padded = assemble(centre, fetch)
        conv = convolve(padded, conv_weight)
        summed = raw.astype(jnp.float32) + conv + time_shift[None, :, None]
        hidden_state = (mask[:, None, :].astype(jnp.float32) * summed).astype(jnp.bfloat16)
        return (hidden_state, reduce_resolution(hidden_state, stride_weight, coarse_bias))
    hidden_state, octant_list = lax.map(one_block, jnp.arange(total_bricks // block, dtype=jnp.int32))
    hidden_state = hidden_state.reshape(total_bricks, channels, 512)
    octant_list = octant_list.reshape(total_bricks, -1)
    placed = jnp.zeros_like(octant_list).at[coarse_map.astype(jnp.int32)].set(octant_list)
    return (hidden_state, assemble_coarse(placed, total_bricks // 8))
```

```python
import jax
import jax.numpy as jnp
from jax import lax
from jax.experimental import pallas as pl
from jax.experimental.pallas import tpu as pltpu
from jax.sharding import PartitionSpec as P

BF = jnp.bfloat16
F32 = jnp.float32
EPS = 1e-06
BRK = 8
CH = 64
CH2 = 128
VOX = 512
LANES = 128
TAPS = 9

ROLLS = (0, 64, 8, 120, 72, 56)
PLAIN, SWAP, UP, DOWN, SWAP_UP, SWAP_DOWN = range(6)


def column(row):
    n = row.shape[1]
    wide = jnp.broadcast_to(row, (n, n))
    on = lax.broadcasted_iota(jnp.int32, (n, n), 0) == lax.broadcasted_iota(jnp.int32, (n, n), 1)
    return jnp.sum(jnp.where(on, wide, 0.0), axis=1, keepdims=True)


def activate(x, occupied, gain):
    scale = lax.rsqrt(jnp.mean(x * x, axis=0, keepdims=True) + EPS)
    normed = x * scale * gain
    return (normed * jax.nn.sigmoid(normed) * occupied).astype(BF)


def position(dx, dy, dz):
    place = 9 * (dx + 1) + 3 * (dy + 1) + (dz + 1)
    return place - 1 if place > 13 else place


def slot(nb_ref, brick, dx, dy, dz):
    target = nb_ref[brick, position(dx, dy, dz)]
    return jnp.where(target < 0, BRK, target & (BRK - 1))


def lane_masks():
    lane = lax.broadcasted_iota(jnp.int32, (CH, LANES), 1)
    z = lane & 7
    y = (lane >> 3) & 7
    return z == 0, z == 7, y == 0, y == 7, lane < 64


def shifted(take, masks):
    z0, z7, y0, y7, _ = masks
    centre = take(PLAIN, 0, 0)
    edge = jnp.where(y0, take(SWAP, 1, 0), take(SWAP, -1, 0))
    edge_up = jnp.where(y0, take(SWAP_UP, -1, 1), take(SWAP_UP, 1, 1))
    edge_down = jnp.where(y7, take(SWAP_DOWN, 1, -1), take(SWAP_DOWN, -1, -1))
    middle = {
        -1: pltpu.roll(jnp.where(z7, take(DOWN, 0, -1), centre), 1, 1),
        0: centre,
        1: pltpu.roll(jnp.where(z0, take(UP, 0, 1), centre), 127, 1),
    }
    edges = {
        -1: pltpu.roll(jnp.where(z7, edge_down, edge), 1, 1),
        0: edge,
        1: pltpu.roll(jnp.where(z0, edge_up, edge), 127, 1),
    }
    out = []
    for b in (-1, 0, 1):
        for c in (-1, 0, 1):
            if b == -1:
                out.append(pltpu.roll(jnp.where(y7, edges[c], middle[c]), 8, 1))
            elif b == 0:
                out.append(middle[c])
            else:
                out.append(pltpu.roll(jnp.where(y0, edges[c], middle[c]), 120, 1))
    return out


def faces_kernel(low_ref, high_ref, occ_low_ref, occ_high_ref, gain_ref, down_ref, up_ref):
    gain = column(gain_ref[...])
    for source, occ, target in ((low_ref, occ_low_ref, down_ref), (high_ref, occ_high_ref, up_ref)):
        for i in range(BRK):
            occupied = occ[i : i + 1, :].astype(F32)
            target[i] = activate(source[i].astype(F32), occupied, gain)


def inner_kernel(
    nb_ref, features_ref, occ_ref, gain_ref, shift_ref, weight_ref, base_ref, acts, wide, stack
):
    gain = column(gain_ref[...])
    shift = column(shift_ref[...])
    masks = lane_masks()
    low = lax.broadcasted_iota(jnp.int32, (CH, LANES), 1) < 64
    for kind in range(len(ROLLS)):
        acts[kind, BRK] = jnp.zeros((CH, VOX), BF)
    for i in range(BRK):
        occupied = occ_ref[i : i + 1, :].astype(F32)
        active = activate(features_ref[i].astype(F32), occupied, gain)
        acts[PLAIN, i] = active
        for j in range(4):
            cols = slice(j * LANES, (j + 1) * LANES)
            for kind in range(1, len(ROLLS)):
                acts[kind, i, :, cols] = pltpu.roll(active[:, cols], ROLLS[kind], 1)
    for a in range(3):
        wide[a * CH : (a + 1) * CH, :] = (
            weight_ref[TAPS * a : TAPS * (a + 1)].reshape(TAPS * CH, CH).T
        )
    for i in range(BRK):
        slots = {
            (dy, dz): i if (dy, dz) == (0, 0) else slot(nb_ref, i, 0, dy, dz)
            for dy in (-1, 0, 1)
            for dz in (-1, 0, 1)
        }
        for j in range(4):
            cols = slice(j * LANES, (j + 1) * LANES)
            pieces = shifted(lambda kind, dy, dz: acts[kind, slots[dy, dz], :, cols], masks)
            for tap, piece in enumerate(pieces):
                stack[i % 2, tap * CH : (tap + 1) * CH, cols] = piece
        y = jnp.dot(wide[...], stack[i % 2], preferred_element_type=F32)
        for j in range(4):
            cols = slice(j * LANES, (j + 1) * LANES)
            before = slice((j - 1) * LANES, j * LANES)
            after = slice((j + 1) * LANES, (j + 2) * LANES)
            to_high = y[2 * CH :, cols]
            if j > 0:
                to_high = to_high + y[:CH, before]
            to_low = y[:CH, cols]
            if j < 3:
                to_low = to_low + y[2 * CH :, after]
            moved = pltpu.roll(jnp.where(low, to_low, to_high), 64, 1)
            total = y[CH : 2 * CH, cols] + moved + features_ref[i, :, cols].astype(F32) + shift
            base_ref[i, :, cols] = total


def outer_kernel(
    nb_ref,
    map_ref,
    dev_ref,
    base_ref,
    up_ref,
    down_ref,
    occ_ref,
    weight_ref,
    stride_ref,
    bias_ref,
    fine_ref,
    stay_ref,
    leave_ref,
    halo,
    wide,
    wide2,
    stack,
    picked,
    placing,
):
    masks = lane_masks()
    low = masks[4]
    low32 = lax.broadcasted_iota(jnp.int32, (CH, LANES), 1) < 64
    for side, source in ((0, down_ref), (1, up_ref)):
        for kind, roll in enumerate(ROLLS):
            halo[side, kind, BRK] = jnp.zeros((CH, LANES), BF)
            for i in range(BRK):
                face = source[i]
                halo[side, kind, i] = pltpu.roll(face, roll, 1) if roll else face
    for row, a in enumerate((0, 2)):
        wide[row * CH : (row + 1) * CH, :] = (
            weight_ref[TAPS * a : TAPS * (a + 1)].reshape(TAPS * CH, CH).T
        )
    wide2[...] = stride_ref[...].reshape(8 * CH, CH2).T
    for i in range(BRK):

        def take(kind, dy, dz):
            beyond = halo[0, kind, slot(nb_ref, i, 1, dy, dz)]
            ahead = halo[1, kind, slot(nb_ref, i, -1, dy, dz)]
            if kind in (SWAP, SWAP_UP, SWAP_DOWN):
                first, second = ahead, beyond
            else:
                first, second = beyond, ahead
            if kind in (UP, SWAP_UP):
                return first, second
            return first, second

        def merged(kind, dy, dz):
            first, second = take(kind, dy, dz)
            return jnp.where(split[kind], first, second)

        lane = lax.broadcasted_iota(jnp.int32, (CH, LANES), 1)
        split = {}
        for kind, roll in enumerate(ROLLS):
            moved = 8 if kind in (UP, SWAP_UP) else (-8 if kind in (DOWN, SWAP_DOWN) else 0)
            split[kind] = ((lane - moved) & 127) < 64
        pieces = shifted(merged, masks)
        for tap, piece in enumerate(pieces):
            stack[tap * CH : (tap + 1) * CH, i * LANES : (i + 1) * LANES] = piece
    edge = jnp.dot(wide[...], stack[...], preferred_element_type=F32)
    for i in range(BRK):
        cols = slice(i * LANES, (i + 1) * LANES)
        moved = pltpu.roll(jnp.where(low32, edge[CH:, cols], edge[:CH, cols]), 64, 1)
        for j in range(4):
            cols = slice(j * LANES, (j + 1) * LANES)
            total = base_ref[i, :, cols]
            if j == 0:
                total = total + jnp.where(low32, moved, 0.0)
            if j == 3:
                total = total + jnp.where(low32, 0.0, moved)
            fine = (occ_ref[i : i + 1, cols].astype(F32) * total).astype(BF)
            fine_ref[i, :, cols] = fine

    source = lax.broadcasted_iota(jnp.int32, (VOX, VOX), 0)
    lane = lax.broadcasted_iota(jnp.int32, (VOX, VOX), 1)
    tap = lane >> 6
    wanted = (
        (2 * ((lane >> 4) & 3) + ((tap >> 2) & 1)) * 64
        + (2 * ((lane >> 2) & 3) + ((tap >> 1) & 1)) * 8
        + 2 * (lane & 3)
        + (tap & 1)
    )
    select = (source == wanted).astype(BF)
    for pair in range(BRK // 2):
        both = fine_ref[2 * pair : 2 * pair + 2].reshape(2 * CH, VOX)
        sorted_ = jnp.dot(both, select, preferred_element_type=F32).astype(BF)
        first, second = sorted_[:CH], sorted_[CH:]
        for j in range(4):
            cols = slice(j * LANES, (j + 1) * LANES)
            one, two = first[:, cols], second[:, cols]
            target = slice(pair * LANES, (pair + 1) * LANES)
            picked[2 * j * CH : (2 * j + 1) * CH, target] = jnp.where(
                low, one, pltpu.roll(two, 64, 1)
            )
            picked[(2 * j + 1) * CH : (2 * j + 2) * CH, target] = jnp.where(
                low, pltpu.roll(one, 64, 1), two
            )
    octant = jnp.dot(wide2[...], picked[...], preferred_element_type=F32)
    octant = (octant + column(bias_ref[...])).astype(BF)

    entry = lax.broadcasted_iota(jnp.int32, (CH, VOX), 0)
    voxel = lax.broadcasted_iota(jnp.int32, (CH, VOX), 1)
    from_entry = ((voxel >> 6) & 3) * 16 + ((voxel >> 3) & 3) * 4 + (voxel & 3)
    of_octant = ((voxel >> 8) & 1) * 4 + ((voxel >> 5) & 1) * 2 + ((voxel >> 2) & 1)
    hit = jnp.where(entry == from_entry, of_octant, -1)
    for i in range(BRK):
        target = map_ref[i]
        stays = (target >> 3) == dev_ref[0]
        which = target & 7
        rows = slice(i * CH, (i + 1) * CH)
        placing[rows, :VOX] = (hit == jnp.where(stays, which, 8)).astype(BF)
        placing[rows, VOX:] = (hit == jnp.where(stays, 8, which)).astype(BF)
    placed = jnp.dot(octant, placing[...], preferred_element_type=F32).astype(BF)
    stay_ref[...] = placed[:, :VOX]
    leave_ref[...] = placed[:, VOX:]


def shards(
    features,
    occupancy,
    neighbours,
    coarse_map,
    norm_gain,
    time_shift,
    conv_weight,
    stride_weight,
    coarse_bias,
):
    groups = lax.axis_size("grp")
    total = lax.axis_size("bricks") * groups
    device = lax.axis_index("bricks") * groups + lax.axis_index("grp")
    vmem = pl.BlockSpec(memory_space=pltpu.VMEM)
    smem = pl.BlockSpec(memory_space=pltpu.SMEM)
    gain = norm_gain.reshape(1, CH)
    shift = time_shift.reshape(1, CH)
    bias = coarse_bias.reshape(1, CH2)

    faces = jax.ShapeDtypeStruct((BRK, CH, LANES), BF)
    down, up = pl.pallas_call(
        faces_kernel,
        grid=(1,),
        in_specs=[
            pl.BlockSpec((BRK, CH, LANES), lambda i: (0, 0, 0)),
            pl.BlockSpec((BRK, CH, LANES), lambda i: (0, 0, 3)),
            pl.BlockSpec((BRK, LANES), lambda i: (0, 0)),
            pl.BlockSpec((BRK, LANES), lambda i: (0, 3)),
            pl.BlockSpec((1, CH), lambda i: (0, 0)),
        ],
        out_specs=[pl.BlockSpec((BRK, CH, LANES), lambda i: (0, 0, 0))] * 2,
        out_shape=(faces, faces),
        name="faces",
    )(features, features, occupancy, occupancy, gain)

    pairs = [(i, i + 1) for i in range(total - 1)]
    from_below = lax.ppermute(up, ("bricks", "grp"), pairs)
    from_above = lax.ppermute(down, ("bricks", "grp"), [(j, i) for i, j in pairs])

    base = pl.pallas_call(
        inner_kernel,
        in_specs=[smem, vmem, vmem, vmem, vmem, vmem],
        out_specs=vmem,
        out_shape=jax.ShapeDtypeStruct((BRK, CH, VOX), F32),
        scratch_shapes=[
            pltpu.VMEM((len(ROLLS), BRK + 1, CH, VOX), BF),
            pltpu.VMEM((3 * CH, TAPS * CH), BF),
            pltpu.VMEM((2, TAPS * CH, VOX), BF),
        ],
        compiler_params=pltpu.CompilerParams(vmem_limit_bytes=24 << 20),
        cost_estimate=pl.CostEstimate(
            flops=2 * 27 * CH * CH * VOX * BRK, bytes_accessed=2 << 20, transcendentals=0
        ),
        name="inner",
    )(neighbours, features, occupancy, gain, shift, conv_weight)

    fine, stay, leave = pl.pallas_call(
        outer_kernel,
        in_specs=[smem, smem, smem] + [vmem] * 7,
        out_specs=[vmem] * 3,
        out_shape=(
            jax.ShapeDtypeStruct((BRK, CH, VOX), BF),
            jax.ShapeDtypeStruct((CH2, VOX), BF),
            jax.ShapeDtypeStruct((CH2, VOX), BF),
        ),
        scratch_shapes=[
            pltpu.VMEM((2, len(ROLLS), BRK + 1, CH, LANES), BF),
            pltpu.VMEM((2 * CH, TAPS * CH), BF),
            pltpu.VMEM((CH2, 8 * CH), BF),
            pltpu.VMEM((TAPS * CH, BRK * LANES), BF),
            pltpu.VMEM((8 * CH, BRK * CH), BF),
            pltpu.VMEM((BRK * CH, 2 * VOX), BF),
        ],
        compiler_params=pltpu.CompilerParams(vmem_limit_bytes=24 << 20),
        name="outer",
    )(
        neighbours,
        coarse_map,
        device.reshape(1).astype(jnp.int32),
        base,
        from_below,
        from_above,
        occupancy,
        conv_weight,
        stride_weight,
        bias,
    )
    arrived = lax.ppermute(leave, "grp", [(i, i ^ 1) for i in range(groups)])
    return fine, (stay + arrived)[None]


def solution(mesh):
    both = ("bricks", "grp")
    return jax.shard_map(
        shards,
        mesh=mesh,
        in_specs=(
            P(both, None, None),
            P(both, None),
            P(both, None),
            P(both),
            P(),
            P(),
            P(),
            P(),
            P(),
        ),
        out_specs=(P(both, None, None), P(both, None, None)),
        check_vma=False,
    )
```

```python
import jax
import jax.numpy as jnp
import ml_dtypes
import numpy as np
from jax import lax
from jax.experimental import pallas as pl
from jax.experimental.pallas import tpu as pltpu
from jax.sharding import PartitionSpec as P

BF = jnp.bfloat16
F32 = jnp.float32
EPS = 1e-06
BRK = 8
CH = 64
CH2 = 128
VOX = 512
LANES = 128
TAPS = 9

LOADED = range(8)

ROLLS = (0, 64, 8, 120, 72, 56)
PLAIN, SWAP, UP, DOWN, SWAP_UP, SWAP_DOWN = range(6)


def column(row):
    n = row.shape[1]
    wide = jnp.broadcast_to(row, (n, n))
    on = lax.broadcasted_iota(jnp.int32, (n, n), 0) == lax.broadcasted_iota(jnp.int32, (n, n), 1)
    return jnp.sum(jnp.where(on, wide, 0.0), axis=1, keepdims=True)


def activate(x, occupied, gain):
    scale = lax.rsqrt(jnp.mean(x * x, axis=0, keepdims=True) + EPS)
    normed = x * scale * gain
    return (normed * jax.nn.sigmoid(normed) * occupied).astype(BF)


def position(dx, dy, dz):
    place = 9 * (dx + 1) + 3 * (dy + 1) + (dz + 1)
    return place - 1 if place > 13 else place


def slot(nb_ref, brick, dx, dy, dz):
    target = nb_ref[brick, position(dx, dy, dz)]
    return jnp.where(target < 0, BRK, target & (BRK - 1))


def lane_masks():
    lane = lax.broadcasted_iota(jnp.int32, (CH, LANES), 1)
    z = lane & 7
    y = (lane >> 3) & 7
    return z == 0, z == 7, y == 0, y == 7, lane < 64


def first_stage(take, masks):
    z0, z7, y0, y7, _ = masks
    centre = take(PLAIN, 0, 0)
    edge = jnp.where(y0, take(SWAP, 1, 0), take(SWAP, -1, 0))
    edge_up = jnp.where(y0, take(SWAP_UP, -1, 1), take(SWAP_UP, 1, 1))
    edge_down = jnp.where(y7, take(SWAP_DOWN, 1, -1), take(SWAP_DOWN, -1, -1))
    middle = (
        pltpu.roll(jnp.where(z7, take(DOWN, 0, -1), centre), 1, 1),
        centre,
        pltpu.roll(jnp.where(z0, take(UP, 0, 1), centre), 127, 1),
    )
    edges = (
        pltpu.roll(jnp.where(z7, edge_down, edge), 1, 1),
        edge,
        pltpu.roll(jnp.where(z0, edge_up, edge), 127, 1),
    )
    return middle, edges


def second_stage(parts, masks, store):
    _, _, y0, y7, _ = masks
    middle, edges = parts
    for c in range(3):
        store(c, pltpu.roll(jnp.where(y7, edges[c], middle[c]), 8, 1))
        store(3 + c, middle[c])
        store(6 + c, pltpu.roll(jnp.where(y0, edges[c], middle[c]), 120, 1))


def halo_stage(raw, masks):
    _, _, y0, _, _ = masks
    edge = pltpu.roll(jnp.where(y0, raw(1, 0), raw(-1, 0)), ROLLS[SWAP], 1)
    edge_up = pltpu.roll(jnp.where(y0, raw(1, 1), raw(-1, 1)), ROLLS[SWAP_UP], 1)
    edge_down = pltpu.roll(jnp.where(y0, raw(1, -1), raw(-1, -1)), ROLLS[SWAP_DOWN], 1)
    up = pltpu.roll(raw(0, 1), ROLLS[UP], 1)
    down = pltpu.roll(raw(0, -1), ROLLS[DOWN], 1)
    return raw(0, 0), edge, edge_up, edge_down, up, down


def halo_second(parts, masks):
    z0, z7, _, _, _ = masks
    centre, edge, edge_up, edge_down, up, down = parts
    middle = (
        pltpu.roll(jnp.where(z7, down, centre), 1, 1),
        centre,
        pltpu.roll(jnp.where(z0, up, centre), 127, 1),
    )
    edges = (
        pltpu.roll(jnp.where(z7, edge_down, edge), 1, 1),
        edge,
        pltpu.roll(jnp.where(z0, edge_up, edge), 127, 1),
    )
    return middle, edges


def columns(j):
    return slice(j * LANES, (j + 1) * LANES)


def faces_kernel(*refs):
    count = len(LOADED)
    sources, face_ref, kept, sems = refs[:count], refs[count], refs[count + 1 : -1], refs[-1]
    copies = [
        pltpu.make_async_copy(source, target, sems.at[k])
        for k, (source, target) in enumerate(zip(sources, kept))
    ]
    for copy in copies:
        copy.start()
    for copy in copies[:3]:
        copy.wait()
    features_ref, occ_ref, gain_ref = kept[:3]
    gain = column(gain_ref[...])
    low = lax.broadcasted_iota(jnp.int32, (CH, LANES), 1) < 64
    for i in range(BRK):
        first, last = features_ref[i, :, columns(0)], features_ref[i, :, columns(3)]
        x = jnp.where(low, first.astype(F32), last.astype(F32))
        row = slice(i, i + 1)
        occupied = jnp.where(low[:1], occ_ref[row, columns(0)], occ_ref[row, columns(3)])
        face_ref[i] = activate(x, occupied.astype(F32), gain)
    for copy in copies[3:]:
        copy.wait()


def inner_kernel(
    nb_ref, features_ref, occ_ref, gain_ref, shift_ref, weight_ref, base_ref,
    acts, wide, stack, ybuf, nb, sem,
):
    copy = pltpu.make_async_copy(nb_ref, nb, sem)
    copy.start()
    gain = column(gain_ref[...])
    shift = column(shift_ref[...])
    masks = lane_masks()
    low = lax.broadcasted_iota(jnp.int32, (CH, LANES), 1) < 64
    for kind in range(len(ROLLS)):
        acts[kind, BRK] = jnp.zeros((CH, VOX), BF)

    def rotate(i):
        for j in range(4):
            piece = acts[PLAIN, i, :, columns(j)]
            for kind in range(1, len(ROLLS)):
                acts[kind, i, :, columns(j)] = pltpu.roll(piece, ROLLS[kind], 1)

    for i in range(BRK):
        occupied = occ_ref[i : i + 1, :].astype(F32)
        acts[PLAIN, i] = activate(features_ref[i].astype(F32), occupied, gain)
        if i > 0:
            rotate(i - 1)
    for a in range(3):
        wide[a * CH : (a + 1) * CH, :] = (
            weight_ref[TAPS * a : TAPS * (a + 1)].reshape(TAPS * CH, CH).T
        )
    rotate(BRK - 1)
    copy.wait()

    def product(i, half):
        lanes = slice(2 * half * LANES, 2 * (half + 1) * LANES)
        ybuf[i % 2, :, lanes] = jnp.dot(
            wide[...], stack[i % 2, :, lanes], preferred_element_type=F32
        )

    def finish(i, half):
        y = ybuf.at[i % 2]
        for j in (2 * half, 2 * half + 1):
            to_high = y[2 * CH :, columns(j)]
            if j > 0:
                to_high = to_high + y[:CH, columns(j - 1)]
            to_low = y[:CH, columns(j)]
            if j < 3:
                to_low = to_low + y[2 * CH :, columns(j + 1)]
            moved = pltpu.roll(jnp.where(low, to_low, to_high), 64, 1)
            total = y[CH : 2 * CH, columns(j)] + features_ref[i, :, columns(j)].astype(F32)
            base_ref[i, :, columns(j)] = (total + shift) + moved

    waiting = None
    for i in range(BRK + 1):
        if i < BRK:
            slots = {
                (dy, dz): i if (dy, dz) == (0, 0) else slot(nb, i, 0, dy, dz)
                for dy in (-1, 0, 1)
                for dz in (-1, 0, 1)
            }
        for j in range(4):
            parts = None
            if i < BRK:
                parts = first_stage(
                    lambda kind, dy, dz: acts[kind, slots[dy, dz], :, columns(j)], masks
                )
            if waiting is not None:
                oi, oj, old = waiting

                def store(tap, piece):
                    stack[oi % 2, tap * CH : (tap + 1) * CH, columns(oj)] = piece

                second_stage(old, masks, store)
                if oj == 1:
                    product(oi, 0)
                if oj == 3:
                    product(oi, 1)
            waiting = (i, j, parts) if parts is not None else None
            if i > 0 and j == 1:
                finish(i - 1, 0)
            if i > 0 and j == 2:
                finish(i - 1, 1)


def outer_kernel(
    nb_ref, map_ref, base_ref, chip_ref, far_ref, occ_ref, weight_ref, stride_ref, bias_ref,
    sort_ref, entry_ref, place_ref,
    fine_ref, stay_ref, leave_ref,
    halo, wide, wide2, stack, picked, placing, mask, nb, map_, order, sems,
):
    copies = [
        pltpu.make_async_copy(nb_ref, nb, sems.at[0]),
        pltpu.make_async_copy(map_ref, map_, sems.at[1]),
    ]
    for copy in copies:
        copy.start()
    groups = lax.axis_size("grp")
    device = lax.axis_index("bricks") * groups + lax.axis_index("grp")
    odd = lax.rem(device, 2)
    masks = lane_masks()
    low = masks[4]
    low32 = lax.broadcasted_iota(jnp.int32, (CH, LANES), 1) < 64
    for i in range(BRK):
        halo[odd, i] = chip_ref[i]
        halo[1 - odd, i] = far_ref[i]
    for i in range(BRK):
        mask[i] = occ_ref[i : i + 1, :].astype(F32)
    halo[0, BRK] = jnp.zeros((CH, LANES), BF)
    halo[1, BRK] = jnp.zeros((CH, LANES), BF)
    for row, a in enumerate((0, 2)):
        wide[row * CH : (row + 1) * CH, :] = (
            weight_ref[TAPS * a : TAPS * (a + 1)].reshape(TAPS * CH, CH).T
        )
    wide2[...] = stride_ref[...].reshape(8 * CH, CH2).T
    for copy in copies:
        copy.wait()
    staying, leaving = jnp.int32(0), jnp.int32(BRK // 2)
    for i in range(BRK):
        stays = (map_[0, i] >> 3) == device
        order[jnp.where(stays, staying, leaving)] = i
        staying = staying + stays.astype(jnp.int32)
        leaving = leaving + 1 - stays.astype(jnp.int32)
    brick = [order[k] for k in range(BRK)]

    def raw_of(i):
        def raw(dy, dz):
            return jnp.where(
                low,
                halo[0, slot(nb, i, 1, dy, dz)],
                halo[1, slot(nb, i, -1, dy, dz)],
            )

        return raw

    def finish(pair):
        lanes = slice(2 * pair * LANES, 2 * (pair + 1) * LANES)
        edge = jnp.dot(wide[...], stack[:, lanes], preferred_element_type=F32)
        for k in range(2):
            i = brick[2 * pair + k]
            mine = edge[:, columns(k)]
            moved = pltpu.roll(jnp.where(low32, mine[CH:], mine[:CH]), 64, 1)
            for j in range(4):
                total = base_ref[i, :, columns(j)]
                if j == 0:
                    total = total + jnp.where(low32, moved, 0.0)
                if j == 3:
                    total = total + jnp.where(low32, 0.0, moved)
                occupied = mask[i, :, columns(j)]
                fine_ref[i, :, columns(j)] = (occupied * total).astype(BF)

    def sort(pair):
        both = jnp.concatenate([fine_ref[brick[2 * pair]], fine_ref[brick[2 * pair + 1]]], axis=0)
        by_tap = jnp.dot(both, sort_ref[...], preferred_element_type=F32).astype(BF)
        for j in range(4):
            one, two = by_tap[:CH, columns(j)], by_tap[CH:, columns(j)]
            picked[2 * j * CH : (2 * j + 1) * CH, columns(pair)] = jnp.where(
                low, one, pltpu.roll(two, 64, 1)
            )
            picked[(2 * j + 1) * CH : (2 * j + 2) * CH, columns(pair)] = jnp.where(
                low, pltpu.roll(one, 64, 1), two
            )

    first, second = None, None
    for k in range(BRK + 2):
        now = halo_stage(raw_of(brick[k]), masks) if k < BRK else None
        later = halo_second(first, masks) if first is not None else None
        if second is not None:
            spot = k - 2

            def store(tap, piece):
                stack[tap * CH : (tap + 1) * CH, columns(spot)] = piece

            second_stage(second, masks, store)
            if spot % 2 == 1:
                finish(spot // 2)
                if spot >= 3:
                    sort(spot // 2 - 1)
        first, second = now, later
    sort(BRK // 2 - 1)
    for k in range(BRK):
        which = map_[0, brick[k]] & 7
        row = place_ref[which].astype(BF)
        placing[k * CH : (k + 1) * CH, :] = entry_ref[...] * row
    octant = jnp.dot(wide2[...], picked[...], preferred_element_type=F32)
    octant = (octant + column(bias_ref[...])).astype(BF)
    half = BRK // 2 * CH
    leave_ref[...] = jnp.dot(
        octant[:, half:], placing[half:, :], preferred_element_type=F32
    ).astype(BF)
    stay_ref[...] = jnp.dot(
        octant[:, :half], placing[:half, :], preferred_element_type=F32
    ).astype(BF)


def tables():
    voxel = np.arange(VOX)
    x, y, z = voxel >> 6, (voxel >> 3) & 7, voxel & 7
    lane = 64 * (4 * (x & 1) + 2 * (y & 1) + (z & 1)) + 16 * (x >> 1) + 4 * (y >> 1) + (z >> 1)
    sort = (lane[:, None] == voxel[None, :]).astype(ml_dtypes.bfloat16)
    source = 16 * (x & 3) + 4 * (y & 3) + (z & 3)
    entry = (np.arange(64)[:, None] == source[None, :]).astype(ml_dtypes.bfloat16)
    octant = 4 * (x >> 2) + 2 * (y >> 2) + (z >> 2)
    place = (np.arange(8)[:, None, None] == octant).astype(np.float32)
    return sort, entry, place


def shards(
    features,
    occupancy,
    neighbours,
    coarse_map,
    norm_gain,
    time_shift,
    conv_weight,
    stride_weight,
    coarse_bias,
):
    groups = lax.axis_size("grp")
    total = lax.axis_size("bricks") * groups
    vmem = pl.BlockSpec(memory_space=pltpu.VMEM)

    loaded = (
        features,
        occupancy,
        norm_gain.reshape(1, CH),
        time_shift.reshape(1, CH),
        conv_weight,
        neighbours,
        coarse_map.reshape(1, BRK),
        coarse_bias.reshape(1, CH2),
    )
    face, features, occupancy, gain, shift, conv_weight, neighbours, coarse_map, bias = (
        pl.pallas_call(
            faces_kernel,
            in_specs=[pl.BlockSpec(memory_space=pltpu.HBM)] * len(loaded),
            out_specs=[vmem] * (1 + len(loaded)),
            out_shape=[jax.ShapeDtypeStruct((BRK, CH, LANES), BF)]
            + [jax.ShapeDtypeStruct(x.shape, x.dtype) for x in loaded],
            scratch_shapes=[pltpu.SemaphoreType.DMA((len(loaded),))],
            compiler_params=pltpu.CompilerParams(vmem_limit_bytes=8 << 20),
            name="faces",
        )(*(pltpu.with_memory_space_constraint(x, pltpu.HBM) for x in loaded))
    )

    chip = lax.ppermute(face, "grp", [(i, i ^ 1) for i in range(groups)])
    across = [(i, i + 1) for i in range(1, total - 1, 2)]
    far = lax.ppermute(face, ("bricks", "grp"), across + [(j, i) for i, j in across])

    base = pl.pallas_call(
        inner_kernel,
        in_specs=[vmem] * 6,
        out_specs=vmem,
        out_shape=jax.ShapeDtypeStruct((BRK, CH, VOX), F32),
        scratch_shapes=[
            pltpu.VMEM((len(ROLLS), BRK + 1, CH, VOX), BF),
            pltpu.VMEM((3 * CH, TAPS * CH), BF),
            pltpu.VMEM((2, TAPS * CH, VOX), BF),
            pltpu.VMEM((2, 3 * CH, VOX), F32),
            pltpu.SMEM((BRK, 26), jnp.int32),
            pltpu.SemaphoreType.DMA,
        ],
        compiler_params=pltpu.CompilerParams(vmem_limit_bytes=16 << 20),
        cost_estimate=pl.CostEstimate(
            flops=2 * 27 * CH * CH * VOX * BRK, bytes_accessed=2 << 20, transcendentals=0
        ),
        name="inner",
    )(neighbours, features, occupancy, gain, shift, conv_weight)

    sort, entry, place = (jnp.asarray(table) for table in tables())
    fine, stay, leave = pl.pallas_call(
        outer_kernel,
        in_specs=[vmem] * 12,
        out_specs=[vmem] * 3,
        out_shape=(
            jax.ShapeDtypeStruct((BRK, CH, VOX), BF),
            jax.ShapeDtypeStruct((CH2, VOX), BF),
            jax.ShapeDtypeStruct((CH2, VOX), BF),
        ),
        scratch_shapes=[
            pltpu.VMEM((2, BRK + 1, CH, LANES), BF),
            pltpu.VMEM((2 * CH, TAPS * CH), BF),
            pltpu.VMEM((CH2, 8 * CH), BF),
            pltpu.VMEM((TAPS * CH, BRK * LANES), BF),
            pltpu.VMEM((8 * CH, BRK * CH), BF),
            pltpu.VMEM((BRK * CH, VOX), BF),
            pltpu.VMEM((BRK, 1, VOX), F32),
            pltpu.SMEM((BRK, 26), jnp.int32),
            pltpu.SMEM((1, BRK), jnp.int32),
            pltpu.SMEM((BRK,), jnp.int32),
            pltpu.SemaphoreType.DMA((2,)),
        ],
        compiler_params=pltpu.CompilerParams(vmem_limit_bytes=16 << 20),
        name="outer",
    )(
        neighbours,
        coarse_map,
        base,
        chip,
        far,
        occupancy,
        conv_weight,
        stride_weight,
        bias,
        sort,
        entry,
        place,
    )
    arrived = lax.ppermute(leave, "grp", [(i, i ^ 1) for i in range(groups)])
    return fine, (stay + arrived)[None]


def solution(mesh):
    both = ("bricks", "grp")
    return jax.shard_map(
        shards,
        mesh=mesh,
        in_specs=(
            P(both, None, None),
            P(both, None),
            P(both, None),
            P(both),
            P(),
            P(),
            P(),
            P(),
            P(),
        ),
        out_specs=(P(both, None, None), P(both, None, None)),
        check_vma=False,
    )
```

```python
import jax
import jax.numpy as jnp
import ml_dtypes
import numpy as np
from jax import lax
from jax.experimental import pallas as pl
from jax.experimental.pallas import tpu as pltpu
from jax.sharding import PartitionSpec as P

BF = jnp.bfloat16
F32 = jnp.float32
EPS = 1e-06
BRK = 8
CH = 64
CH2 = 128
VOX = 512
LANES = 128
TAPS = 9

LOADED = range(8)

ROLLS = (0, 64, 8, 120, 72, 56)
PLAIN, SWAP, UP, DOWN, SWAP_UP, SWAP_DOWN = range(6)


def column(row):
    n = row.shape[1]
    wide = jnp.broadcast_to(row, (n, n))
    on = lax.broadcasted_iota(jnp.int32, (n, n), 0) == lax.broadcasted_iota(jnp.int32, (n, n), 1)
    return jnp.sum(jnp.where(on, wide, 0.0), axis=1, keepdims=True)


def activate(x, occupied, gain):
    scale = lax.rsqrt(jnp.mean(x * x, axis=0, keepdims=True) + EPS)
    normed = x * scale * gain
    return (normed * jax.nn.sigmoid(normed) * occupied).astype(BF)


def position(dx, dy, dz):
    place = 9 * (dx + 1) + 3 * (dy + 1) + (dz + 1)
    return place - 1 if place > 13 else place


def slot(nb_ref, brick, dx, dy, dz):
    target = nb_ref[brick, position(dx, dy, dz)]
    return jnp.where(target < 0, BRK, target & (BRK - 1))


def lane_masks():
    lane = lax.broadcasted_iota(jnp.int32, (CH, LANES), 1)
    z = lane & 7
    y = (lane >> 3) & 7
    return z == 0, z == 7, y == 0, y == 7, lane < 64


def first_stage(take, masks):
    z0, z7, y0, y7, _ = masks
    centre = take(PLAIN, 0, 0)
    edge = jnp.where(y0, take(SWAP, 1, 0), take(SWAP, -1, 0))
    edge_up = jnp.where(y0, take(SWAP_UP, -1, 1), take(SWAP_UP, 1, 1))
    edge_down = jnp.where(y7, take(SWAP_DOWN, 1, -1), take(SWAP_DOWN, -1, -1))
    middle = (
        pltpu.roll(jnp.where(z7, take(DOWN, 0, -1), centre), 1, 1),
        centre,
        pltpu.roll(jnp.where(z0, take(UP, 0, 1), centre), 127, 1),
    )
    edges = (
        pltpu.roll(jnp.where(z7, edge_down, edge), 1, 1),
        edge,
        pltpu.roll(jnp.where(z0, edge_up, edge), 127, 1),
    )
    return middle, edges


def second_stage(parts, masks, store):
    _, _, y0, y7, _ = masks
    middle, edges = parts
    for c in range(3):
        store(c, pltpu.roll(jnp.where(y7, edges[c], middle[c]), 8, 1))
        store(3 + c, middle[c])
        store(6 + c, pltpu.roll(jnp.where(y0, edges[c], middle[c]), 120, 1))


def halo_stage(raw, masks):
    _, _, y0, _, _ = masks
    edge = pltpu.roll(jnp.where(y0, raw(1, 0), raw(-1, 0)), ROLLS[SWAP], 1)
    edge_up = pltpu.roll(jnp.where(y0, raw(1, 1), raw(-1, 1)), ROLLS[SWAP_UP], 1)
    edge_down = pltpu.roll(jnp.where(y0, raw(1, -1), raw(-1, -1)), ROLLS[SWAP_DOWN], 1)
    up = pltpu.roll(raw(0, 1), ROLLS[UP], 1)
    down = pltpu.roll(raw(0, -1), ROLLS[DOWN], 1)
    return raw(0, 0), edge, edge_up, edge_down, up, down


def halo_second(parts, masks):
    z0, z7, _, _, _ = masks
    centre, edge, edge_up, edge_down, up, down = parts
    middle = (
        pltpu.roll(jnp.where(z7, down, centre), 1, 1),
        centre,
        pltpu.roll(jnp.where(z0, up, centre), 127, 1),
    )
    edges = (
        pltpu.roll(jnp.where(z7, edge_down, edge), 1, 1),
        edge,
        pltpu.roll(jnp.where(z0, edge_up, edge), 127, 1),
    )
    return middle, edges


def columns(j):
    return slice(j * LANES, (j + 1) * LANES)


def faces_kernel(*refs):
    count = len(LOADED)
    sources, face_ref, kept, sems = refs[:count], refs[count], refs[count + 1 : -1], refs[-1]
    copies = [
        pltpu.make_async_copy(source, target, sems.at[k])
        for k, (source, target) in enumerate(zip(sources, kept))
    ]
    for copy in copies:
        copy.start()
    for copy in copies[:3]:
        copy.wait()
    features_ref, occ_ref, gain_ref = kept[:3]
    gain = column(gain_ref[...])
    low = lax.broadcasted_iota(jnp.int32, (CH, LANES), 1) < 64
    for i in range(BRK):
        first, last = features_ref[i, :, columns(0)], features_ref[i, :, columns(3)]
        x = jnp.where(low, first.astype(F32), last.astype(F32))
        row = slice(i, i + 1)
        occupied = jnp.where(low[:1], occ_ref[row, columns(0)], occ_ref[row, columns(3)])
        face_ref[i] = activate(x, occupied.astype(F32), gain)
    for copy in copies[3:]:
        copy.wait()


def inner_kernel(
    nb_ref, features_ref, occ_ref, gain_ref, shift_ref, weight_ref, base_ref,
    acts, wide, stack, ybuf, nb, sem,
):
    copy = pltpu.make_async_copy(nb_ref, nb, sem)
    copy.start()
    gain = column(gain_ref[...])
    shift = column(shift_ref[...])
    masks = lane_masks()
    low = lax.broadcasted_iota(jnp.int32, (CH, LANES), 1) < 64
    for kind in range(len(ROLLS)):
        acts[kind, BRK] = jnp.zeros((CH, VOX), BF)

    def rotate(i):
        for j in range(4):
            piece = acts[PLAIN, i, :, columns(j)]
            for kind in range(1, len(ROLLS)):
                acts[kind, i, :, columns(j)] = pltpu.roll(piece, ROLLS[kind], 1)

    for i in range(BRK):
        occupied = occ_ref[i : i + 1, :].astype(F32)
        acts[PLAIN, i] = activate(features_ref[i].astype(F32), occupied, gain)
        if i > 0:
            rotate(i - 1)
    for a in range(3):
        wide[a * CH : (a + 1) * CH, :] = (
            weight_ref[TAPS * a : TAPS * (a + 1)].reshape(TAPS * CH, CH).T
        )
    rotate(BRK - 1)
    copy.wait()

    def product(i, half):
        lanes = slice(2 * half * LANES, 2 * (half + 1) * LANES)
        ybuf[i % 2, :, lanes] = jnp.dot(
            wide[...], stack[i % 2, :, lanes], preferred_element_type=F32
        )

    def finish(i, half):
        y = ybuf.at[i % 2]
        for j in (2 * half, 2 * half + 1):
            to_high = y[2 * CH :, columns(j)]
            if j > 0:
                to_high = to_high + y[:CH, columns(j - 1)]
            to_low = y[:CH, columns(j)]
            if j < 3:
                to_low = to_low + y[2 * CH :, columns(j + 1)]
            moved = pltpu.roll(jnp.where(low, to_low, to_high), 64, 1)
            total = y[CH : 2 * CH, columns(j)] + features_ref[i, :, columns(j)].astype(F32)
            base_ref[i, :, columns(j)] = (total + shift) + moved

    waiting = None
    for i in range(BRK + 1):
        if i < BRK:
            slots = {
                (dy, dz): i if (dy, dz) == (0, 0) else slot(nb, i, 0, dy, dz)
                for dy in (-1, 0, 1)
                for dz in (-1, 0, 1)
            }
        for j in range(4):
            parts = None
            if i < BRK:
                parts = first_stage(
                    lambda kind, dy, dz: acts[kind, slots[dy, dz], :, columns(j)], masks
                )
            if waiting is not None:
                oi, oj, old = waiting

                def store(tap, piece):
                    stack[oi % 2, tap * CH : (tap + 1) * CH, columns(oj)] = piece

                second_stage(old, masks, store)
            waiting = (i, j, parts) if parts is not None else None
            if i < BRK and j == 3:
                product(i, 0)
            if i > 0 and j == 1:
                product(i - 1, 1)
            if i > 0 and j == 2:
                finish(i - 1, 0)
            if i > 0 and j == 3:
                finish(i - 1, 1)


def outer_kernel(
    nb_ref, map_ref, base_ref, chip_ref, far_ref, occ_ref, weight_ref, stride_ref, bias_ref,
    sort_ref, entry_ref, place_ref,
    fine_hbm, stay_ref, leave_ref,
    fine_ref, halo, wide, wide2, stack, picked, placing, mask, nb, map_, order, sems,
):
    copies = [
        pltpu.make_async_copy(nb_ref, nb, sems.at[0]),
        pltpu.make_async_copy(map_ref, map_, sems.at[1]),
    ]
    for copy in copies:
        copy.start()
    groups = lax.axis_size("grp")
    device = lax.axis_index("bricks") * groups + lax.axis_index("grp")
    odd = lax.rem(device, 2)
    masks = lane_masks()
    low = masks[4]
    low32 = lax.broadcasted_iota(jnp.int32, (CH, LANES), 1) < 64
    for i in range(BRK):
        halo[odd, i] = chip_ref[i]
        halo[1 - odd, i] = far_ref[i]
    for i in range(BRK):
        mask[i] = occ_ref[i : i + 1, :].astype(F32)
    halo[0, BRK] = jnp.zeros((CH, LANES), BF)
    halo[1, BRK] = jnp.zeros((CH, LANES), BF)
    for row, a in enumerate((0, 2)):
        wide[row * CH : (row + 1) * CH, :] = (
            weight_ref[TAPS * a : TAPS * (a + 1)].reshape(TAPS * CH, CH).T
        )
    for c in range(2):
        taps = jnp.concatenate([stride_ref[2 * k + c] for k in range(4)], axis=0)
        wide2[c] = taps.T
    for copy in copies:
        copy.wait()
    staying, leaving = jnp.int32(0), jnp.int32(BRK // 2)
    for i in range(BRK):
        stays = (map_[0, i] >> 3) == device
        order[jnp.where(stays, staying, leaving)] = i
        staying = staying + stays.astype(jnp.int32)
        leaving = leaving + 1 - stays.astype(jnp.int32)
    brick = [order[k] for k in range(BRK)]

    def raw_of(i):
        def raw(dy, dz):
            return jnp.where(
                low,
                halo[0, slot(nb, i, 1, dy, dz)],
                halo[1, slot(nb, i, -1, dy, dz)],
            )

        return raw

    def finish(pair):
        lanes = slice(2 * pair * LANES, 2 * (pair + 1) * LANES)
        edge = jnp.dot(wide[...], stack[:, lanes], preferred_element_type=F32)
        for k in range(2):
            i = brick[2 * pair + k]
            mine = edge[:, columns(k)]
            moved = pltpu.roll(jnp.where(low32, mine[CH:], mine[:CH]), 64, 1)
            for j in range(4):
                total = base_ref[i, :, columns(j)]
                if j == 0:
                    total = total + jnp.where(low32, moved, 0.0)
                if j == 3:
                    total = total + jnp.where(low32, 0.0, moved)
                occupied = mask[i, :, columns(j)]
                fine_ref[i, :, columns(j)] = (occupied * total).astype(BF)

    def sort(half):
        sorted_ = []
        for k in range(2):
            rows = [fine_ref[brick[4 * half + 2 * pair + k]] for pair in range(2)]
            sorted_.append(
                jnp.dot(
                    jnp.concatenate(rows, axis=0), sort_ref[k], preferred_element_type=F32
                ).astype(BF)
            )
        for pair in range(2):
            rows = slice(pair * CH, (pair + 1) * CH)
            for j in range(4):
                one, two = sorted_[0][rows, columns(j)], sorted_[1][rows, columns(j)]
                taps = slice(j * CH, (j + 1) * CH)
                picked[0, taps, columns(2 * half + pair)] = jnp.where(low, one, two)
                picked[1, taps, columns(2 * half + pair)] = jnp.where(low, two, one)

    for k in range(BRK):
        which = map_[0, brick[k]] & 7
        row = place_ref[which].astype(BF)
        placing[k * CH : (k + 1) * CH, :] = entry_ref[...] * row
    first, second = None, None
    for k in range(BRK + 2):
        now = halo_stage(raw_of(brick[k]), masks) if k < BRK else None
        later = halo_second(first, masks) if first is not None else None
        if second is not None:
            spot = k - 2

            def store(tap, piece):
                stack[tap * CH : (tap + 1) * CH, columns(spot)] = piece

            second_stage(second, masks, store)
            if spot % 2 == 1:
                finish(spot // 2)
                if spot == 5:
                    sort(0)
        first, second = now, later
    out = pltpu.make_async_copy(fine_ref, fine_hbm, sems.at[2])
    out.start()
    sort(1)
    octant = []
    for pair in range(BRK // 2):
        even, odd = (
            jnp.dot(wide2[c], picked[c, :, columns(pair)], preferred_element_type=F32)
            for c in range(2)
        )
        octant.append(even + pltpu.roll(odd, 64, 1))
    octant = (jnp.concatenate(octant, axis=1) + column(bias_ref[...])).astype(BF)
    half = BRK // 2 * CH
    leave_ref[...] = jnp.dot(
        octant[:, half:], placing[half:, :], preferred_element_type=F32
    ).astype(BF)
    stay_ref[...] = jnp.dot(
        octant[:, :half], placing[:half, :], preferred_element_type=F32
    ).astype(BF)
    out.wait()


def tables():
    voxel = np.arange(VOX)
    x, y, z = voxel >> 6, (voxel >> 3) & 7, voxel & 7
    lane = 64 * (4 * (x & 1) + 2 * (y & 1) + (z & 1)) + 16 * (x >> 1) + 4 * (y >> 1) + (z >> 1)
    sort = np.stack([lane[:, None] == voxel, (lane ^ 64)[:, None] == voxel]).astype(ml_dtypes.bfloat16)
    source = 16 * (x & 3) + 4 * (y & 3) + (z & 3)
    entry = (np.arange(64)[:, None] == source[None, :]).astype(ml_dtypes.bfloat16)
    octant = 4 * (x >> 2) + 2 * (y >> 2) + (z >> 2)
    place = (np.arange(8)[:, None, None] == octant).astype(np.float32)
    return sort, entry, place


def shards(
    features,
    occupancy,
    neighbours,
    coarse_map,
    norm_gain,
    time_shift,
    conv_weight,
    stride_weight,
    coarse_bias,
):
    groups = lax.axis_size("grp")
    total = lax.axis_size("bricks") * groups
    vmem = pl.BlockSpec(memory_space=pltpu.VMEM)

    loaded = (
        features,
        occupancy,
        norm_gain.reshape(1, CH),
        time_shift.reshape(1, CH),
        conv_weight,
        neighbours,
        coarse_map.reshape(1, BRK),
        coarse_bias.reshape(1, CH2),
    )
    face, features, occupancy, gain, shift, conv_weight, neighbours, coarse_map, bias = (
        pl.pallas_call(
            faces_kernel,
            in_specs=[pl.BlockSpec(memory_space=pltpu.HBM)] * len(loaded),
            out_specs=[vmem] * (1 + len(loaded)),
            out_shape=[jax.ShapeDtypeStruct((BRK, CH, LANES), BF)]
            + [jax.ShapeDtypeStruct(x.shape, x.dtype) for x in loaded],
            scratch_shapes=[pltpu.SemaphoreType.DMA((len(loaded),))],
            compiler_params=pltpu.CompilerParams(vmem_limit_bytes=8 << 20),
            name="faces",
        )(*(pltpu.with_memory_space_constraint(x, pltpu.HBM) for x in loaded))
    )

    chip = lax.ppermute(face, "grp", [(i, i ^ 1) for i in range(groups)])
    across = [(i, i + 1) for i in range(1, total - 1, 2)]
    far = lax.ppermute(face, ("bricks", "grp"), across + [(j, i) for i, j in across])

    base = pl.pallas_call(
        inner_kernel,
        in_specs=[vmem] * 6,
        out_specs=vmem,
        out_shape=jax.ShapeDtypeStruct((BRK, CH, VOX), F32),
        scratch_shapes=[
            pltpu.VMEM((len(ROLLS), BRK + 1, CH, VOX), BF),
            pltpu.VMEM((3 * CH, TAPS * CH), BF),
            pltpu.VMEM((2, TAPS * CH, VOX), BF),
            pltpu.VMEM((2, 3 * CH, VOX), F32),
            pltpu.SMEM((BRK, 26), jnp.int32),
            pltpu.SemaphoreType.DMA,
        ],
        compiler_params=pltpu.CompilerParams(vmem_limit_bytes=16 << 20),
        cost_estimate=pl.CostEstimate(
            flops=2 * 27 * CH * CH * VOX * BRK, bytes_accessed=2 << 20, transcendentals=0
        ),
        name="inner",
    )(neighbours, features, occupancy, gain, shift, conv_weight)

    sort, entry, place = (jnp.asarray(table) for table in tables())
    fine, stay, leave = pl.pallas_call(
        outer_kernel,
        in_specs=[vmem] * 12,
        out_specs=[pl.BlockSpec(memory_space=pltpu.HBM), vmem, vmem],
        out_shape=(
            jax.ShapeDtypeStruct((BRK, CH, VOX), BF),
            jax.ShapeDtypeStruct((CH2, VOX), BF),
            jax.ShapeDtypeStruct((CH2, VOX), BF),
        ),
        scratch_shapes=[
            pltpu.VMEM((BRK, CH, VOX), BF),
            pltpu.VMEM((2, BRK + 1, CH, LANES), BF),
            pltpu.VMEM((2 * CH, TAPS * CH), BF),
            pltpu.VMEM((2, CH2, 4 * CH), BF),
            pltpu.VMEM((TAPS * CH, BRK * LANES), BF),
            pltpu.VMEM((2, 4 * CH, BRK * CH), BF),
            pltpu.VMEM((BRK * CH, VOX), BF),
            pltpu.VMEM((BRK, 1, VOX), F32),
            pltpu.SMEM((BRK, 26), jnp.int32),
            pltpu.SMEM((1, BRK), jnp.int32),
            pltpu.SMEM((BRK,), jnp.int32),
            pltpu.SemaphoreType.DMA((3,)),
        ],
        compiler_params=pltpu.CompilerParams(vmem_limit_bytes=16 << 20),
        name="outer",
    )(
        neighbours,
        coarse_map,
        base,
        chip,
        far,
        occupancy,
        conv_weight,
        stride_weight,
        bias,
        sort,
        entry,
        place,
    )
    arrived = lax.ppermute(leave, "grp", [(i, i ^ 1) for i in range(groups)])
    return fine, (stay + arrived)[None]


def solution(mesh):
    both = ("bricks", "grp")
    return jax.shard_map(
        shards,
        mesh=mesh,
        in_specs=(
            P(both, None, None),
            P(both, None),
            P(both, None),
            P(both),
            P(),
            P(),
            P(),
            P(),
            P(),
        ),
        out_specs=(P(both, None, None), P(both, None, None)),
        check_vma=False,
    )
```

```python
import functools

import jax
import jax.numpy as jnp
import ml_dtypes
import numpy as np
from jax import lax
from jax.experimental import pallas as pl
from jax.experimental.pallas import tpu as pltpu
from jax.sharding import PartitionSpec as P

BF = jnp.bfloat16
F32 = jnp.float32
EPS = 1e-06
BRK = 8
CH = 64
CH2 = 128
VOX = 512
LANES = 128
TAPS = 9

LOADED = 8
HALF = BRK // 2

ROLLS = (0, 64, 8, 120, 72, 56)
PLAIN, SWAP, UP, DOWN, SWAP_UP, SWAP_DOWN = range(6)


def column(row):
    n = row.shape[1]
    wide = jnp.broadcast_to(row, (n, n))
    on = lax.broadcasted_iota(jnp.int32, (n, n), 0) == lax.broadcasted_iota(jnp.int32, (n, n), 1)
    return jnp.sum(jnp.where(on, wide, 0.0), axis=1, keepdims=True)


def activate(x, occupied, gain):
    scale = lax.rsqrt(jnp.mean(x * x, axis=0, keepdims=True) + EPS)
    normed = x * scale * gain
    return (normed * jax.nn.sigmoid(normed) * occupied).astype(BF)


def position(dx, dy, dz):
    place = 9 * (dx + 1) + 3 * (dy + 1) + (dz + 1)
    return place - 1 if place > 13 else place


def slot(nb_ref, brick, dx, dy, dz):
    target = nb_ref[brick, position(dx, dy, dz)]
    return jnp.where(target < 0, BRK, target & (BRK - 1))


def lane_masks():
    lane = lax.broadcasted_iota(jnp.int32, (CH, LANES), 1)
    z = lane & 7
    y = (lane >> 3) & 7
    return z == 0, z == 7, y == 0, y == 7, lane < 64


def first_stage(take, masks):
    z0, z7, y0, y7, _ = masks
    centre = take(PLAIN, 0, 0)
    edge = jnp.where(y0, take(SWAP, 1, 0), take(SWAP, -1, 0))
    edge_up = jnp.where(y0, take(SWAP_UP, -1, 1), take(SWAP_UP, 1, 1))
    edge_down = jnp.where(y7, take(SWAP_DOWN, 1, -1), take(SWAP_DOWN, -1, -1))
    middle = (
        pltpu.roll(jnp.where(z7, take(DOWN, 0, -1), centre), 1, 1),
        centre,
        pltpu.roll(jnp.where(z0, take(UP, 0, 1), centre), 127, 1),
    )
    edges = (
        pltpu.roll(jnp.where(z7, edge_down, edge), 1, 1),
        edge,
        pltpu.roll(jnp.where(z0, edge_up, edge), 127, 1),
    )
    return middle, edges


def second_stage(parts, masks, store):
    _, _, y0, y7, _ = masks
    middle, edges = parts
    for c in range(3):
        store(c, pltpu.roll(jnp.where(y7, edges[c], middle[c]), 8, 1))
        store(3 + c, middle[c])
        store(6 + c, pltpu.roll(jnp.where(y0, edges[c], middle[c]), 120, 1))


def halo_stage(raw, masks):
    _, _, y0, _, _ = masks
    edge = pltpu.roll(jnp.where(y0, raw(1, 0), raw(-1, 0)), ROLLS[SWAP], 1)
    edge_up = pltpu.roll(jnp.where(y0, raw(1, 1), raw(-1, 1)), ROLLS[SWAP_UP], 1)
    edge_down = pltpu.roll(jnp.where(y0, raw(1, -1), raw(-1, -1)), ROLLS[SWAP_DOWN], 1)
    up = pltpu.roll(raw(0, 1), ROLLS[UP], 1)
    down = pltpu.roll(raw(0, -1), ROLLS[DOWN], 1)
    return raw(0, 0), edge, edge_up, edge_down, up, down


def halo_second(parts, masks):
    z0, z7, _, _, _ = masks
    centre, edge, edge_up, edge_down, up, down = parts
    middle = (
        pltpu.roll(jnp.where(z7, down, centre), 1, 1),
        centre,
        pltpu.roll(jnp.where(z0, up, centre), 127, 1),
    )
    edges = (
        pltpu.roll(jnp.where(z7, edge_down, edge), 1, 1),
        edge,
        pltpu.roll(jnp.where(z0, edge_up, edge), 127, 1),
    )
    return middle, edges


def columns(j):
    return slice(j * LANES, (j + 1) * LANES)


def faces_kernel(*refs):
    count = LOADED
    sources, face_ref, kept, sems = refs[:count], refs[count], refs[count + 1 : -1], refs[-1]
    copies = [
        pltpu.make_async_copy(source, target, sems.at[k])
        for k, (source, target) in enumerate(zip(sources, kept))
    ]
    for copy in copies:
        copy.start()
    for copy in copies[:3]:
        copy.wait()
    features_ref, occ_ref, gain_ref = kept[:3]
    gain = column(gain_ref[...])
    low = lax.broadcasted_iota(jnp.int32, (CH, LANES), 1) < 64
    for i in range(BRK):
        first, last = features_ref[i, :, columns(0)], features_ref[i, :, columns(3)]
        x = jnp.where(low, first.astype(F32), last.astype(F32))
        row = slice(i, i + 1)
        occupied = jnp.where(low[:1], occ_ref[row, columns(0)], occ_ref[row, columns(3)])
        face_ref[i] = activate(x, occupied.astype(F32), gain)
    for copy in copies[3:]:
        copy.wait()


def inner_kernel(
    nb_ref, features_ref, occ_ref, gain_ref, shift_ref, weight_ref, edge_ref, middle_ref, wide,
    acts, stack, ybuf, nb, sem,
):
    copy = pltpu.make_async_copy(nb_ref, nb, sem)
    copy.start()
    gain = column(gain_ref[...])
    shift = column(shift_ref[...])
    masks = lane_masks()
    low = lax.broadcasted_iota(jnp.int32, (CH, LANES), 1) < 64
    for kind in range(len(ROLLS)):
        acts[kind, BRK] = jnp.zeros((CH, VOX), BF)

    def rotate(i):
        for j in range(4):
            piece = acts[PLAIN, i, :, columns(j)]
            for kind in range(1, len(ROLLS)):
                acts[kind, i, :, columns(j)] = pltpu.roll(piece, ROLLS[kind], 1)

    for i in range(BRK):
        occupied = occ_ref[i : i + 1, :].astype(F32)
        acts[PLAIN, i] = activate(features_ref[i].astype(F32), occupied, gain)
        if i > 0:
            rotate(i - 1)
    for a in range(3):
        wide[a * CH : (a + 1) * CH, :] = (
            weight_ref[TAPS * a : TAPS * (a + 1)].reshape(TAPS * CH, CH).T
        )
    rotate(BRK - 1)
    copy.wait()

    def product(i, half):
        lanes = slice(2 * half * LANES, 2 * (half + 1) * LANES)
        ybuf[i % 2, :, lanes] = jnp.dot(
            wide[...], stack[i % 2, :, lanes], preferred_element_type=F32
        )

    def finish(i, half):
        y = ybuf.at[i % 2]
        for j in (2 * half, 2 * half + 1):
            to_high = y[2 * CH :, columns(j)]
            if j > 0:
                to_high = to_high + y[:CH, columns(j - 1)]
            to_low = y[:CH, columns(j)]
            if j < 3:
                to_low = to_low + y[2 * CH :, columns(j + 1)]
            moved = pltpu.roll(jnp.where(low, to_low, to_high), 64, 1)
            total = y[CH : 2 * CH, columns(j)] + features_ref[i, :, columns(j)].astype(F32)
            total = occ_ref[i : i + 1, columns(j)].astype(F32) * ((total + shift) + moved)
            if j in (0, 3):
                edge_ref[i, :, columns(j // 3)] = total
            else:
                middle_ref[i, :, columns(j - 1)] = total.astype(BF)

    waiting = None
    for i in range(BRK + 1):
        if i < BRK:
            slots = {
                (dy, dz): i if (dy, dz) == (0, 0) else slot(nb, i, 0, dy, dz)
                for dy in (-1, 0, 1)
                for dz in (-1, 0, 1)
            }
        for j in range(4):
            parts = None
            if i < BRK:
                parts = first_stage(
                    lambda kind, dy, dz: acts[kind, slots[dy, dz], :, columns(j)], masks
                )
            if waiting is not None:
                oi, oj, old = waiting

                def store(tap, piece):
                    stack[oi % 2, tap * CH : (tap + 1) * CH, columns(oj)] = piece

                second_stage(old, masks, store)
            waiting = (i, j, parts) if parts is not None else None
            if i < BRK and j == 3:
                product(i, 0)
            if i > 0 and j == 1:
                product(i - 1, 1)
            if i > 0 and j == 2:
                finish(i - 1, 0)
            if i > 0 and j == 3:
                finish(i - 1, 1)


def sorted_voxels(rows, sort_ref, picked, low):
    sorted_ = [
        jnp.dot(
            jnp.concatenate([rows[k], rows[2 + k]], axis=0),
            sort_ref[k],
            preferred_element_type=F32,
        ).astype(BF)
        for k in range(2)
    ]
    for pair in range(2):
        part = slice(pair * CH, (pair + 1) * CH)
        for j in range(4):
            one, two = sorted_[0][part, columns(j)], sorted_[1][part, columns(j)]
            taps = slice(j * CH, (j + 1) * CH)
            picked[0, taps, columns(pair)] = jnp.where(low, one, two)
            picked[1, taps, columns(pair)] = jnp.where(low, two, one)


def octants(wide2, picked, bias):
    even, odd = (jnp.dot(wide2[c], picked[c], preferred_element_type=F32) for c in range(2))
    both = [
        even[:, columns(pair)] + pltpu.roll(odd[:, columns(pair)], 64, 1) for pair in range(2)
    ]
    return (jnp.concatenate(both, axis=1) + bias).astype(BF)


def outer_kernel(
    nb_ref, map_ref, edge_ref, middle_ref, chip_ref, far_ref, occ_ref, wide, stride_ref, bias_ref,
    sort_ref, entry_ref, place_ref,
    ends_ref, rows_ref, placing_ref, wide2, leave_ref,
    halo, stack, picked, placing, mask, faces, leaving_ends, nb, map_, order, sems,
):
    copies = [
        pltpu.make_async_copy(nb_ref, nb, sems.at[0]),
        pltpu.make_async_copy(map_ref, map_, sems.at[1]),
    ]
    for copy in copies:
        copy.start()
    groups = lax.axis_size("grp")
    device = lax.axis_index("bricks") * groups + lax.axis_index("grp")
    odd = lax.rem(device, 2)
    masks = lane_masks()
    low = masks[4]
    low32 = lax.broadcasted_iota(jnp.int32, (CH, LANES), 1) < 64
    for i in range(BRK):
        halo[odd, i] = chip_ref[i]
        halo[1 - odd, i] = far_ref[i]
        row = slice(i, i + 1)
        mask[i] = jnp.where(
            low32[:1], occ_ref[row, columns(0)], occ_ref[row, columns(3)]
        ).astype(F32)
    halo[0, BRK] = jnp.zeros((CH, LANES), BF)
    halo[1, BRK] = jnp.zeros((CH, LANES), BF)
    for c in range(2):
        taps = jnp.concatenate([stride_ref[2 * k + c] for k in range(4)], axis=0)
        wide2[c] = taps.T
    bias = column(bias_ref[...])
    for copy in copies:
        copy.wait()
    leaving, staying = jnp.int32(0), jnp.int32(HALF)
    for i in range(BRK):
        stays = (map_[0, i] >> 3) == device
        order[jnp.where(stays, staying, leaving)] = i
        staying = staying + stays.astype(jnp.int32)
        leaving = leaving + 1 - stays.astype(jnp.int32)
    brick = [order[k] for k in range(BRK)]

    def raw_of(i):
        def raw(dy, dz):
            return jnp.where(
                low,
                halo[0, slot(nb, i, 1, dy, dz)],
                halo[1, slot(nb, i, -1, dy, dz)],
            )

        return raw

    def product(pair):
        lanes = slice(2 * pair * LANES, 2 * (pair + 1) * LANES)
        ends = jnp.concatenate([wide[:CH], wide[2 * CH :]], axis=0)
        faces[:, lanes] = jnp.dot(ends, stack[:, lanes], preferred_element_type=F32)

    def finish(k):
        i = brick[k]
        mine = faces[:, columns(k)]
        moved = pltpu.roll(jnp.where(low32, mine[CH:], mine[:CH]), 64, 1) * mask[i]
        for side in range(2):
            keep = low32 if side == 0 else jnp.logical_not(low32)
            fine = (edge_ref[i, :, columns(side)] + jnp.where(keep, moved, 0.0)).astype(BF)
            ends_ref[i, :, columns(side)] = fine
            if k < HALF:
                leaving_ends[k, :, columns(side)] = fine
            else:
                rows_ref[k - HALF, :, columns(2 + side)] = fine
        if k >= HALF:
            rows_ref[k - HALF, :, : 2 * LANES] = middle_ref[i]

    def place(k, target):
        which = map_[0, brick[k]] & 7
        part = slice(k % HALF * CH, (k % HALF + 1) * CH)
        target[part, :] = entry_ref[...] * place_ref[which].astype(BF)

    for k in range(HALF):
        place(k, placing)
        place(HALF + k, placing_ref)
    first, second, result = None, None, None
    for k in range(BRK + 2):
        now = halo_stage(raw_of(brick[k]), masks) if k < BRK else None
        later = halo_second(first, masks) if first is not None else None
        if second is not None:
            spot = k - 2

            def store(tap, piece):
                stack[tap * CH : (tap + 1) * CH, columns(spot)] = piece

            second_stage(second, masks, store)
            if spot == 2 or spot == 4 or spot == 6:
                finish(spot - 2)
                finish(spot - 1)
            if spot % 2 == 1:
                product(spot // 2)
            if spot == 5:
                rows = [
                    jnp.concatenate([middle_ref[brick[q]], leaving_ends[q]], axis=1)
                    for q in range(HALF)
                ]
                sorted_voxels(rows, sort_ref, picked, low)
            if spot == 6:
                result = octants(wide2, picked, bias)
            if spot == 7:
                leave_ref[...] = jnp.dot(
                    result, placing[...], preferred_element_type=F32
                ).astype(BF)
        first, second = now, later
    finish(BRK - 2)
    finish(BRK - 1)


def staying_kernel(
    ends_ref, middle_ref, rows_ref, placing_ref, wide2, sort_ref, bias_ref,
    fine_hbm, stay_ref, picked, sems,
):
    copies = [
        pltpu.make_async_copy(middle_ref, fine_hbm.at[:, :, LANES : 3 * LANES], sems.at[0])
    ] + [
        pltpu.make_async_copy(
            ends_ref.at[:, :, columns(side)], fine_hbm.at[:, :, columns(3 * side)], sems.at[1 + side]
        )
        for side in range(2)
    ]
    for copy in copies:
        copy.start()
    low = lane_masks()[4]
    sorted_voxels([rows_ref[k] for k in range(HALF)], sort_ref, picked, low)
    octant = octants(wide2, picked, column(bias_ref[...]))
    stay_ref[...] = jnp.dot(octant, placing_ref[...], preferred_element_type=F32).astype(BF)
    for copy in copies:
        copy.wait()


def tables():
    voxel = np.arange(VOX)
    x, y, z = voxel >> 6, (voxel >> 3) & 7, voxel & 7
    lane = 64 * (4 * (x & 1) + 2 * (y & 1) + (z & 1)) + 16 * (x >> 1) + 4 * (y >> 1) + (z >> 1)
    sort = np.stack([lane[:, None] == voxel, (lane ^ 64)[:, None] == voxel])
    sort = sort.reshape(2, 4, LANES, VOX)[:, [1, 2, 0, 3]].reshape(2, VOX, VOX)
    sort = sort.astype(ml_dtypes.bfloat16)
    source = 16 * (x & 3) + 4 * (y & 3) + (z & 3)
    entry = (np.arange(64)[:, None] == source[None, :]).astype(ml_dtypes.bfloat16)
    octant = 4 * (x >> 2) + 2 * (y >> 2) + (z >> 2)
    place = (np.arange(8)[:, None, None] == octant).astype(np.float32)
    return sort, entry, place


def shards(
    features,
    occupancy,
    neighbours,
    coarse_map,
    norm_gain,
    time_shift,
    conv_weight,
    stride_weight,
    coarse_bias,
):
    groups = lax.axis_size("grp")
    total = lax.axis_size("bricks") * groups
    vmem = pl.BlockSpec(memory_space=pltpu.VMEM)

    loaded = (
        features,
        occupancy,
        norm_gain.reshape(1, CH),
        time_shift.reshape(1, CH),
        conv_weight,
        neighbours,
        coarse_map.reshape(1, BRK),
        coarse_bias.reshape(1, CH2),
    )
    face, features, occupancy, gain, shift, conv_weight, neighbours, coarse_map, bias = (
        pl.pallas_call(
            faces_kernel,
            in_specs=[pl.BlockSpec(memory_space=pltpu.HBM)] * len(loaded),
            out_specs=[vmem] * (1 + len(loaded)),
            out_shape=[jax.ShapeDtypeStruct((BRK, CH, LANES), BF)]
            + [jax.ShapeDtypeStruct(x.shape, x.dtype) for x in loaded],
            scratch_shapes=[pltpu.SemaphoreType.DMA((len(loaded),))],
            compiler_params=pltpu.CompilerParams(vmem_limit_bytes=8 << 20),
            name="faces",
        )(*(pltpu.with_memory_space_constraint(x, pltpu.HBM) for x in loaded))
    )

    chip = lax.ppermute(face, "grp", [(i, i ^ 1) for i in range(groups)])
    across = [(i, i + 1) for i in range(1, total - 1, 2)]
    far = lax.ppermute(face, ("bricks", "grp"), across + [(j, i) for i, j in across])

    edge, middle, wide = pl.pallas_call(
        inner_kernel,
        in_specs=[vmem] * 6,
        out_specs=[vmem] * 3,
        out_shape=(
            jax.ShapeDtypeStruct((BRK, CH, 2 * LANES), F32),
            jax.ShapeDtypeStruct((BRK, CH, 2 * LANES), BF),
            jax.ShapeDtypeStruct((3 * CH, TAPS * CH), BF),
        ),
        scratch_shapes=[
            pltpu.VMEM((len(ROLLS), BRK + 1, CH, VOX), BF),
            pltpu.VMEM((2, TAPS * CH, VOX), BF),
            pltpu.VMEM((2, 3 * CH, VOX), F32),
            pltpu.SMEM((BRK, 26), jnp.int32),
            pltpu.SemaphoreType.DMA,
        ],
        compiler_params=pltpu.CompilerParams(vmem_limit_bytes=16 << 20),
        cost_estimate=pl.CostEstimate(
            flops=2 * 27 * CH * CH * VOX * BRK, bytes_accessed=2 << 20, transcendentals=0
        ),
        name="inner",
    )(neighbours, features, occupancy, gain, shift, conv_weight)

    sort, entry, place = (jnp.asarray(table) for table in tables())
    placed = jax.ShapeDtypeStruct((CH2, VOX), BF)
    ends, rows, placing, wide2, leave = pl.pallas_call(
        outer_kernel,
        in_specs=[vmem] * 13,
        out_specs=[vmem] * 5,
        out_shape=(
            jax.ShapeDtypeStruct((BRK, CH, 2 * LANES), BF),
            jax.ShapeDtypeStruct((HALF, CH, VOX), BF),
            jax.ShapeDtypeStruct((HALF * CH, VOX), BF),
            jax.ShapeDtypeStruct((2, CH2, 4 * CH), BF),
            placed,
        ),
        scratch_shapes=[
            pltpu.VMEM((2, BRK + 1, CH, LANES), BF),
            pltpu.VMEM((TAPS * CH, BRK * LANES), BF),
            pltpu.VMEM((2, 4 * CH, HALF * CH), BF),
            pltpu.VMEM((HALF * CH, VOX), BF),
            pltpu.VMEM((BRK, 1, LANES), F32),
            pltpu.VMEM((2 * CH, BRK * LANES), F32),
            pltpu.VMEM((HALF, CH, 2 * LANES), BF),
            pltpu.SMEM((BRK, 26), jnp.int32),
            pltpu.SMEM((1, BRK), jnp.int32),
            pltpu.SMEM((BRK,), jnp.int32),
            pltpu.SemaphoreType.DMA((2,)),
        ],
        compiler_params=pltpu.CompilerParams(vmem_limit_bytes=16 << 20),
        name="outer",
    )(
        neighbours,
        coarse_map,
        edge,
        middle,
        chip,
        far,
        occupancy,
        wide,
        stride_weight,
        bias,
        sort,
        entry,
        place,
    )
    arrived = lax.ppermute(leave, "grp", [(i, i ^ 1) for i in range(groups)])
    fine, stay = pl.pallas_call(
        staying_kernel,
        in_specs=[vmem] * 7,
        out_specs=[pl.BlockSpec(memory_space=pltpu.HBM), vmem],
        out_shape=(jax.ShapeDtypeStruct((BRK, CH, VOX), BF), placed),
        scratch_shapes=[
            pltpu.VMEM((2, 4 * CH, HALF * CH), BF),
            pltpu.SemaphoreType.DMA((3,)),
        ],
        compiler_params=pltpu.CompilerParams(vmem_limit_bytes=8 << 20),
        cost_estimate=pl.CostEstimate(
            flops=2 * 8 * CH * CH2 * VOX * HALF, bytes_accessed=2 << 20, transcendentals=0
        ),
        name="staying",
    )(ends, middle, rows, placing, wide2, sort, bias)
    return fine, (stay + arrived)[None]


def solution(mesh):
    both = ("bricks", "grp")
    return jax.shard_map(
        shards,
        mesh=mesh,
        in_specs=(
            P(both, None, None),
            P(both, None),
            P(both, None),
            P(both),
            P(),
            P(),
            P(),
            P(),
            P(),
        ),
        out_specs=(P(both, None, None), P(both, None, None)),
        check_vma=False,
    )
```

```python
import functools

import jax
import jax.numpy as jnp
import ml_dtypes
import numpy as np
from jax import lax
from jax.experimental import pallas as pl
from jax.experimental.pallas import tpu as pltpu
from jax.sharding import PartitionSpec as P

BF = jnp.bfloat16
F32 = jnp.float32
EPS = 1e-06
BRK = 8
CH = 64
CH2 = 128
VOX = 512
LANES = 128
TAPS = 9

LOADED = 8
HALF = BRK // 2

ROLLS = (0, 64, 8, 120, 72, 56)
PLAIN, SWAP, UP, DOWN, SWAP_UP, SWAP_DOWN = range(6)


def column(row):
    n = row.shape[1]
    wide = jnp.broadcast_to(row, (n, n))
    on = lax.broadcasted_iota(jnp.int32, (n, n), 0) == lax.broadcasted_iota(jnp.int32, (n, n), 1)
    return jnp.sum(jnp.where(on, wide, 0.0), axis=1, keepdims=True)


def activate(x, occupied, gain):
    scale = lax.rsqrt(jnp.mean(x * x, axis=0, keepdims=True) + EPS)
    normed = x * scale * gain
    return (normed * jax.nn.sigmoid(normed) * occupied).astype(BF)


def position(dx, dy, dz):
    place = 9 * (dx + 1) + 3 * (dy + 1) + (dz + 1)
    return place - 1 if place > 13 else place


def slot(nb_ref, brick, dx, dy, dz):
    target = nb_ref[brick, position(dx, dy, dz)]
    return jnp.where(target < 0, BRK, target & (BRK - 1))


def lane_masks():
    lane = lax.broadcasted_iota(jnp.int32, (CH, LANES), 1)
    z = lane & 7
    y = (lane >> 3) & 7
    return (z == 0, z == 7), {row: y == row for row in (0, 1, 6, 7)}, lane < 64


def merged(take, masks):
    (z0, z7), y, _ = masks
    centre = take(PLAIN, 0, 0)
    up, down = take(UP, 0, 1), take(DOWN, 0, -1)
    above = jnp.where(y[0], take(SWAP, 1, 0), centre)
    below = jnp.where(y[7], take(SWAP, -1, 0), centre)
    return (
        jnp.where(z7, jnp.where(y[6], take(SWAP_DOWN, -1, -1), down), below),
        below,
        jnp.where(z0, jnp.where(y[0], take(SWAP_UP, -1, 1), up), below),
        jnp.where(z7, down, centre),
        centre,
        jnp.where(z0, up, centre),
        jnp.where(z7, jnp.where(y[7], take(SWAP_DOWN, 1, -1), down), above),
        above,
        jnp.where(z0, jnp.where(y[1], take(SWAP_UP, 1, 1), up), above),
    )


def rotated(sources):
    return [
        pltpu.roll(source, turn, 1) if turn else source
        for source, turn in zip(sources, (9, 8, 7, 1, 0, 127, 121, 120, 119))
    ]


def side_by_side(first, second):
    return jnp.concatenate(
        [jnp.concatenate([one, two], axis=1) for one, two in zip(first, second)], axis=0
    )


def halo_take(raw):
    def take(kind, dy, dz):
        piece = raw(dy, dz)
        return pltpu.roll(piece, ROLLS[kind], 1) if ROLLS[kind] else piece

    return take


def columns(j):
    return slice(j * LANES, (j + 1) * LANES)


def faces_kernel(*refs):
    count = LOADED
    sources, face_ref, kept, sems = refs[:count], refs[count], refs[count + 1 : -1], refs[-1]
    copies = [
        pltpu.make_async_copy(source, target, sems.at[k])
        for k, (source, target) in enumerate(zip(sources, kept))
    ]
    for copy in copies:
        copy.start()
    for copy in copies[:3]:
        copy.wait()
    features_ref, occ_ref, gain_ref = kept[:3]
    gain = column(gain_ref[...])
    low = lax.broadcasted_iota(jnp.int32, (CH, LANES), 1) < 64
    for i in range(BRK):
        first, last = features_ref[i, :, columns(0)], features_ref[i, :, columns(3)]
        x = jnp.where(low, first.astype(F32), last.astype(F32))
        row = slice(i, i + 1)
        occupied = jnp.where(low[:1], occ_ref[row, columns(0)], occ_ref[row, columns(3)])
        face_ref[i] = activate(x, occupied.astype(F32), gain)
    for copy in copies[3:]:
        copy.wait()


def inner_kernel(
    nb_ref, features_ref, occ_ref, gain_ref, shift_ref, weight_ref, edge_ref, middle_ref, wide,
    acts, ybuf, nb, sem,
):
    copy = pltpu.make_async_copy(nb_ref, nb, sem)
    copy.start()
    gain = column(gain_ref[...])
    shift = column(shift_ref[...])
    masks = lane_masks()
    low = lax.broadcasted_iota(jnp.int32, (CH, LANES), 1) < 64
    for kind in range(len(ROLLS)):
        acts[kind, BRK] = jnp.zeros((CH, VOX), BF)

    def rotate(i):
        for j in range(4):
            piece = acts[PLAIN, i, :, columns(j)]
            for kind in range(1, len(ROLLS)):
                acts[kind, i, :, columns(j)] = pltpu.roll(piece, ROLLS[kind], 1)

    for i in range(BRK):
        occupied = occ_ref[i : i + 1, :].astype(F32)
        acts[PLAIN, i] = activate(features_ref[i].astype(F32), occupied, gain)
        if i > 0:
            rotate(i - 1)
    for a in range(3):
        wide[a * CH : (a + 1) * CH, :] = (
            weight_ref[TAPS * a : TAPS * (a + 1)].reshape(TAPS * CH, CH).T
        )
    rotate(BRK - 1)
    copy.wait()

    def product(i, half, first, second):
        lanes = slice(2 * half * LANES, 2 * (half + 1) * LANES)
        ybuf[i % 2, :, lanes] = jnp.dot(
            wide[...], side_by_side(first, second), preferred_element_type=F32
        )

    def finish(i, half):
        y = ybuf.at[i % 2]
        for j in (2 * half, 2 * half + 1):
            to_high = y[2 * CH :, columns(j)]
            if j > 0:
                to_high = to_high + y[:CH, columns(j - 1)]
            to_low = y[:CH, columns(j)]
            if j < 3:
                to_low = to_low + y[2 * CH :, columns(j + 1)]
            moved = pltpu.roll(jnp.where(low, to_low, to_high), 64, 1)
            total = y[CH : 2 * CH, columns(j)] + features_ref[i, :, columns(j)].astype(F32)
            total = occ_ref[i : i + 1, columns(j)].astype(F32) * ((total + shift) + moved)
            if j in (0, 3):
                edge_ref[i, :, columns(j // 3)] = total
            else:
                middle_ref[i, :, columns(j - 1)] = total.astype(BF)

    for i in range(BRK):
        slots = {
            (dy, dz): i if (dy, dz) == (0, 0) else slot(nb, i, 0, dy, dz)
            for dy in (-1, 0, 1)
            for dz in (-1, 0, 1)
        }
        pieces = []
        for j in range(4):
            pieces.append(
                rotated(
                    merged(lambda kind, dy, dz: acts[kind, slots[dy, dz], :, columns(j)], masks)
                )
            )
            if j % 2 == 1:
                product(i, j // 2, *pieces[-2:])
            if i > 0 and j == 0:
                finish(i - 1, 0)
            if i > 0 and j == 2:
                finish(i - 1, 1)
    finish(BRK - 1, 0)
    finish(BRK - 1, 1)


def sorted_voxels(rows, sort_ref, picked, low):
    sorted_ = [
        jnp.dot(
            jnp.concatenate([rows[k], rows[2 + k]], axis=0),
            sort_ref[k],
            preferred_element_type=F32,
        ).astype(BF)
        for k in range(2)
    ]
    for pair in range(2):
        part = slice(pair * CH, (pair + 1) * CH)
        for j in range(4):
            one, two = sorted_[0][part, columns(j)], sorted_[1][part, columns(j)]
            taps = slice(j * CH, (j + 1) * CH)
            picked[0, taps, columns(pair)] = jnp.where(low, one, two)
            picked[1, taps, columns(pair)] = jnp.where(low, two, one)


def octants(wide2, picked, bias):
    even, odd = (jnp.dot(wide2[c], picked[c], preferred_element_type=F32) for c in range(2))
    both = [
        even[:, columns(pair)] + pltpu.roll(odd[:, columns(pair)], 64, 1) for pair in range(2)
    ]
    return (jnp.concatenate(both, axis=1) + bias).astype(BF)


def outer_kernel(
    nb_ref, map_ref, edge_ref, middle_ref, chip_ref, far_ref, occ_ref, wide, stride_ref, bias_ref,
    sort_ref, entry_ref, place_ref,
    ends_ref, rows_ref, placing_ref, wide2, leave_ref,
    halo, picked, mask, faces, leaving_ends, nb, map_, order, sems,
):
    copies = [
        pltpu.make_async_copy(nb_ref, nb, sems.at[0]),
        pltpu.make_async_copy(map_ref, map_, sems.at[1]),
    ]
    for copy in copies:
        copy.start()
    groups = lax.axis_size("grp")
    device = lax.axis_index("bricks") * groups + lax.axis_index("grp")
    odd = lax.rem(device, 2)
    masks = lane_masks()
    low = masks[2]
    low32 = lax.broadcasted_iota(jnp.int32, (CH, LANES), 1) < 64
    for i in range(BRK):
        halo[odd, i] = chip_ref[i]
        halo[1 - odd, i] = far_ref[i]
        row = slice(i, i + 1)
        mask[i] = jnp.where(
            low32[:1], occ_ref[row, columns(0)], occ_ref[row, columns(3)]
        ).astype(F32)
    halo[0, BRK] = jnp.zeros((CH, LANES), BF)
    halo[1, BRK] = jnp.zeros((CH, LANES), BF)
    for c in range(2):
        taps = jnp.concatenate([stride_ref[2 * k + c] for k in range(4)], axis=0)
        wide2[c] = taps.T
    bias = column(bias_ref[...])
    for copy in copies:
        copy.wait()
    leaving, staying = jnp.int32(0), jnp.int32(HALF)
    for i in range(BRK):
        stays = (map_[0, i] >> 3) == device
        order[jnp.where(stays, staying, leaving)] = i
        staying = staying + stays.astype(jnp.int32)
        leaving = leaving + 1 - stays.astype(jnp.int32)
    brick = [order[k] for k in range(BRK)]

    def raw_of(i):
        def raw(dy, dz):
            return jnp.where(
                low,
                halo[0, slot(nb, i, 1, dy, dz)],
                halo[1, slot(nb, i, -1, dy, dz)],
            )

        return raw

    def product(pair, one, two):
        lanes = slice(2 * pair * LANES, 2 * (pair + 1) * LANES)
        ends = jnp.concatenate([wide[:CH], wide[2 * CH :]], axis=0)
        faces[:, lanes] = jnp.dot(ends, side_by_side(one, two), preferred_element_type=F32)

    def finish(k):
        i = brick[k]
        mine = faces[:, columns(k)]
        moved = pltpu.roll(jnp.where(low32, mine[CH:], mine[:CH]), 64, 1) * mask[i]
        for side in range(2):
            keep = low32 if side == 0 else jnp.logical_not(low32)
            fine = (edge_ref[i, :, columns(side)] + jnp.where(keep, moved, 0.0)).astype(BF)
            ends_ref[i, :, columns(side)] = fine
            if k < HALF:
                leaving_ends[k, :, columns(side)] = fine
            else:
                rows_ref[k - HALF, :, columns(2 + side)] = fine
        if k >= HALF:
            rows_ref[k - HALF, :, : 2 * LANES] = middle_ref[i]

    def place(k):
        return entry_ref[...] * place_ref[map_[0, brick[k]] & 7].astype(BF)

    for k in range(HALF):
        placing_ref[k * CH : (k + 1) * CH, :] = place(HALF + k)
    before, result, pieces = None, None, []
    for k in range(BRK + 1):
        now = merged(halo_take(raw_of(brick[k])), masks) if k < BRK else None
        if before is not None:
            spot = k - 1
            pieces.append(rotated(before))
            if spot == 2 or spot == 4 or spot == 6:
                finish(spot - 2)
                finish(spot - 1)
            if spot % 2 == 1:
                product(spot // 2, *pieces[-2:])
            if spot == 5:
                rows = [
                    jnp.concatenate([middle_ref[brick[q]], leaving_ends[q]], axis=1)
                    for q in range(HALF)
                ]
                sorted_voxels(rows, sort_ref, picked, low)
            if spot == 6:
                result = octants(wide2, picked, bias)
            if spot == 7:
                leave_ref[...] = jnp.dot(
                    result,
                    jnp.concatenate([place(q) for q in range(HALF)], axis=0),
                    preferred_element_type=F32,
                ).astype(BF)
        before = now
    finish(BRK - 2)
    finish(BRK - 1)


def staying_kernel(
    ends_ref, middle_ref, rows_ref, placing_ref, wide2, sort_ref, bias_ref,
    fine_hbm, stay_ref, picked, sems,
):
    copies = [
        pltpu.make_async_copy(middle_ref, fine_hbm.at[:, :, LANES : 3 * LANES], sems.at[0])
    ] + [
        pltpu.make_async_copy(
            ends_ref.at[:, :, columns(side)], fine_hbm.at[:, :, columns(3 * side)], sems.at[1 + side]
        )
        for side in range(2)
    ]
    for copy in copies:
        copy.start()
    low = lane_masks()[2]
    sorted_voxels([rows_ref[k] for k in range(HALF)], sort_ref, picked, low)
    octant = octants(wide2, picked, column(bias_ref[...]))
    stay_ref[...] = jnp.dot(octant, placing_ref[...], preferred_element_type=F32).astype(BF)
    for copy in copies:
        copy.wait()


def tables():
    voxel = np.arange(VOX)
    x, y, z = voxel >> 6, (voxel >> 3) & 7, voxel & 7
    lane = 64 * (4 * (x & 1) + 2 * (y & 1) + (z & 1)) + 16 * (x >> 1) + 4 * (y >> 1) + (z >> 1)
    sort = np.stack([lane[:, None] == voxel, (lane ^ 64)[:, None] == voxel])
    sort = sort.reshape(2, 4, LANES, VOX)[:, [1, 2, 0, 3]].reshape(2, VOX, VOX)
    sort = sort.astype(ml_dtypes.bfloat16)
    source = 16 * (x & 3) + 4 * (y & 3) + (z & 3)
    entry = (np.arange(64)[:, None] == source[None, :]).astype(ml_dtypes.bfloat16)
    octant = 4 * (x >> 2) + 2 * (y >> 2) + (z >> 2)
    place = (np.arange(8)[:, None, None] == octant).astype(np.float32)
    return sort, entry, place


def shards(
    features,
    occupancy,
    neighbours,
    coarse_map,
    norm_gain,
    time_shift,
    conv_weight,
    stride_weight,
    coarse_bias,
):
    groups = lax.axis_size("grp")
    total = lax.axis_size("bricks") * groups
    vmem = pl.BlockSpec(memory_space=pltpu.VMEM)

    loaded = (
        features,
        occupancy,
        norm_gain.reshape(1, CH),
        time_shift.reshape(1, CH),
        conv_weight,
        neighbours,
        coarse_map.reshape(1, BRK),
        coarse_bias.reshape(1, CH2),
    )
    face, features, occupancy, gain, shift, conv_weight, neighbours, coarse_map, bias = (
        pl.pallas_call(
            faces_kernel,
            in_specs=[pl.BlockSpec(memory_space=pltpu.HBM)] * len(loaded),
            out_specs=[vmem] * (1 + len(loaded)),
            out_shape=[jax.ShapeDtypeStruct((BRK, CH, LANES), BF)]
            + [jax.ShapeDtypeStruct(x.shape, x.dtype) for x in loaded],
            scratch_shapes=[pltpu.SemaphoreType.DMA((len(loaded),))],
            compiler_params=pltpu.CompilerParams(vmem_limit_bytes=8 << 20),
            name="faces",
        )(*(pltpu.with_memory_space_constraint(x, pltpu.HBM) for x in loaded))
    )

    chip = lax.ppermute(face, "grp", [(i, i ^ 1) for i in range(groups)])
    across = [(i, i + 1) for i in range(1, total - 1, 2)]
    far = lax.ppermute(face, ("bricks", "grp"), across + [(j, i) for i, j in across])

    edge, middle, wide = pl.pallas_call(
        inner_kernel,
        in_specs=[vmem] * 6,
        out_specs=[vmem] * 3,
        out_shape=(
            jax.ShapeDtypeStruct((BRK, CH, 2 * LANES), F32),
            jax.ShapeDtypeStruct((BRK, CH, 2 * LANES), BF),
            jax.ShapeDtypeStruct((3 * CH, TAPS * CH), BF),
        ),
        scratch_shapes=[
            pltpu.VMEM((len(ROLLS), BRK + 1, CH, VOX), BF),
            pltpu.VMEM((2, 3 * CH, VOX), F32),
            pltpu.SMEM((BRK, 26), jnp.int32),
            pltpu.SemaphoreType.DMA,
        ],
        compiler_params=pltpu.CompilerParams(vmem_limit_bytes=16 << 20),
        cost_estimate=pl.CostEstimate(
            flops=2 * 27 * CH * CH * VOX * BRK, bytes_accessed=2 << 20, transcendentals=0
        ),
        name="inner",
    )(neighbours, features, occupancy, gain, shift, conv_weight)

    sort, entry, place = (jnp.asarray(table) for table in tables())
    placed = jax.ShapeDtypeStruct((CH2, VOX), BF)
    ends, rows, placing, wide2, leave = pl.pallas_call(
        outer_kernel,
        in_specs=[vmem] * 13,
        out_specs=[vmem] * 5,
        out_shape=(
            jax.ShapeDtypeStruct((BRK, CH, 2 * LANES), BF),
            jax.ShapeDtypeStruct((HALF, CH, VOX), BF),
            jax.ShapeDtypeStruct((HALF * CH, VOX), BF),
            jax.ShapeDtypeStruct((2, CH2, 4 * CH), BF),
            placed,
        ),
        scratch_shapes=[
            pltpu.VMEM((2, BRK + 1, CH, LANES), BF),
            pltpu.VMEM((2, 4 * CH, HALF * CH), BF),
            pltpu.VMEM((BRK, 1, LANES), F32),
            pltpu.VMEM((2 * CH, BRK * LANES), F32),
            pltpu.VMEM((HALF, CH, 2 * LANES), BF),
            pltpu.SMEM((BRK, 26), jnp.int32),
            pltpu.SMEM((1, BRK), jnp.int32),
            pltpu.SMEM((BRK,), jnp.int32),
            pltpu.SemaphoreType.DMA((2,)),
        ],
        compiler_params=pltpu.CompilerParams(vmem_limit_bytes=16 << 20),
        name="outer",
    )(
        neighbours,
        coarse_map,
        edge,
        middle,
        chip,
        far,
        occupancy,
        wide,
        stride_weight,
        bias,
        sort,
        entry,
        place,
    )
    arrived = lax.ppermute(leave, "grp", [(i, i ^ 1) for i in range(groups)])
    fine, stay = pl.pallas_call(
        staying_kernel,
        in_specs=[vmem] * 7,
        out_specs=[pl.BlockSpec(memory_space=pltpu.HBM), vmem],
        out_shape=(jax.ShapeDtypeStruct((BRK, CH, VOX), BF), placed),
        scratch_shapes=[
            pltpu.VMEM((2, 4 * CH, HALF * CH), BF),
            pltpu.SemaphoreType.DMA((3,)),
        ],
        compiler_params=pltpu.CompilerParams(vmem_limit_bytes=8 << 20),
        cost_estimate=pl.CostEstimate(
            flops=2 * 8 * CH * CH2 * VOX * HALF, bytes_accessed=2 << 20, transcendentals=0
        ),
        name="staying",
    )(ends, middle, rows, placing, wide2, sort, bias)
    return fine, (stay + arrived)[None]


def solution(mesh):
    both = ("bricks", "grp")
    return jax.shard_map(
        shards,
        mesh=mesh,
        in_specs=(
            P(both, None, None),
            P(both, None),
            P(both, None),
            P(both),
            P(),
            P(),
            P(),
            P(),
            P(),
        ),
        out_specs=(P(both, None, None), P(both, None, None)),
        check_vma=False,
    )
```

```python
import functools

import jax
import jax.numpy as jnp
import ml_dtypes
import numpy as np
from jax import lax
from jax.experimental import pallas as pl
from jax.experimental.pallas import tpu as pltpu
from jax.sharding import PartitionSpec as P

BF = jnp.bfloat16
F32 = jnp.float32
EPS = 1e-06
BRK = 8
CH = 64
CH2 = 128
VOX = 512
LANES = 128
TAPS = 9

LOADED = 8
HALF = BRK // 2

ROLLS = (0, 64, 8, 120, 72, 56)
PLAIN, SWAP, UP, DOWN, SWAP_UP, SWAP_DOWN = range(6)


def column(row):
    n = row.shape[1]
    wide = jnp.broadcast_to(row, (n, n))
    on = lax.broadcasted_iota(jnp.int32, (n, n), 0) == lax.broadcasted_iota(jnp.int32, (n, n), 1)
    return jnp.sum(jnp.where(on, wide, 0.0), axis=1, keepdims=True)


def scale_of(x):
    return lax.rsqrt(jnp.mean(x * x, axis=0, keepdims=True) + EPS)


def activate(x, scale, occupied, gain):
    normed = x * scale * gain
    return (normed * jax.nn.sigmoid(normed) * occupied).astype(BF)


def position(dx, dy, dz):
    place = 9 * (dx + 1) + 3 * (dy + 1) + (dz + 1)
    return place - 1 if place > 13 else place


def slot(nb_ref, brick, dx, dy, dz):
    target = nb_ref[brick, position(dx, dy, dz)]
    return jnp.where(target < 0, BRK, target & (BRK - 1))


def lane_masks():
    lane = lax.broadcasted_iota(jnp.int32, (CH, LANES), 1)
    z = lane & 7
    y = (lane >> 3) & 7
    return (z == 0, z == 7), {row: y == row for row in (0, 1, 6, 7)}, lane < 64


def merged(take, masks):
    (z0, z7), y, _ = masks
    centre = take(PLAIN, 0, 0)
    up, down = take(UP, 0, 1), take(DOWN, 0, -1)
    above = jnp.where(y[0], take(SWAP, 1, 0), centre)
    below = jnp.where(y[7], take(SWAP, -1, 0), centre)
    return (
        jnp.where(z7, jnp.where(y[6], take(SWAP_DOWN, -1, -1), down), below),
        below,
        jnp.where(z0, jnp.where(y[0], take(SWAP_UP, -1, 1), up), below),
        jnp.where(z7, down, centre),
        centre,
        jnp.where(z0, up, centre),
        jnp.where(z7, jnp.where(y[7], take(SWAP_DOWN, 1, -1), down), above),
        above,
        jnp.where(z0, jnp.where(y[1], take(SWAP_UP, 1, 1), up), above),
    )


def rotated(sources):
    return [
        pltpu.roll(source, turn, 1) if turn else source
        for source, turn in zip(sources, (9, 8, 7, 1, 0, 127, 121, 120, 119))
    ]


def side_by_side(*parts):
    return jnp.concatenate([jnp.concatenate(row, axis=1) for row in zip(*parts)], axis=0)


def halo_take(raw):
    def take(kind, dy, dz):
        piece = raw(dy, dz)
        return pltpu.roll(piece, ROLLS[kind], 1) if ROLLS[kind] else piece

    return take


def columns(j):
    return slice(j * LANES, (j + 1) * LANES)


def faces_kernel(*refs):
    count = LOADED
    sources, face_ref, kept, sems = refs[:count], refs[count], refs[count + 1 : -1], refs[-1]
    copies = [
        pltpu.make_async_copy(source, target, sems.at[k])
        for k, (source, target) in enumerate(zip(sources, kept))
    ]
    for copy in copies:
        copy.start()
    for copy in copies[:3]:
        copy.wait()
    features_ref, occ_ref, gain_ref = kept[:3]
    gain = column(gain_ref[...])
    low = lax.broadcasted_iota(jnp.int32, (CH, LANES), 1) < 64
    for i in range(BRK):
        first, last = features_ref[i, :, columns(0)], features_ref[i, :, columns(3)]
        x = jnp.where(low, first.astype(F32), last.astype(F32))
        row = slice(i, i + 1)
        occupied = jnp.where(low[:1], occ_ref[row, columns(0)], occ_ref[row, columns(3)])
        face_ref[i] = activate(x, scale_of(x), occupied.astype(F32), gain)
    for copy in copies[3:]:
        copy.wait()


def inner_kernel(
    nb_ref, features_ref, occ_ref, gain_ref, shift_ref, weight_ref, edge_ref, middle_ref, wide,
    acts, ybuf, nb, sem,
):
    copy = pltpu.make_async_copy(nb_ref, nb, sem)
    copy.start()
    gain = column(gain_ref[...])
    shift = column(shift_ref[...])
    masks = lane_masks()
    low = lax.broadcasted_iota(jnp.int32, (CH, LANES), 1) < 64
    for kind in range(len(ROLLS)):
        acts[kind, BRK] = jnp.zeros((CH, VOX), BF)

    lane = lax.broadcasted_iota(jnp.int32, (LANES, 2 * LANES), 1)
    turn = jnp.where(lane < LANES, ROLLS[SWAP_UP], ROLLS[SWAP_DOWN])
    origin = lax.broadcasted_iota(jnp.int32, (LANES, 2 * LANES), 0)
    turns = (origin == ((lane - turn) & (LANES - 1))).astype(F32).astype(BF)

    def rotate(i):
        for j in range(4):
            piece = acts[PLAIN, i, :, columns(j)]
            for kind in (SWAP, UP, DOWN):
                acts[kind, i, :, columns(j)] = pltpu.roll(piece, ROLLS[kind], 1)
        rows = jnp.concatenate([acts[PLAIN, i, :, columns(j)] for j in range(4)], axis=0)
        both = jnp.dot(rows, turns, preferred_element_type=F32).astype(BF)
        for j in range(4):
            for k, kind in enumerate((SWAP_UP, SWAP_DOWN)):
                acts[kind, i, :, columns(j)] = both[j * CH : (j + 1) * CH, columns(k)]

    scale = scale_of(features_ref[0].astype(F32))
    for i in range(BRK):
        upcoming = scale_of(features_ref[i + 1].astype(F32)) if i + 1 < BRK else None
        occupied = occ_ref[i : i + 1, :].astype(F32)
        acts[PLAIN, i] = activate(features_ref[i].astype(F32), scale, occupied, gain)
        if i > 0:
            rotate(i - 1)
        scale = upcoming
    for a in range(3):
        wide[a * CH : (a + 1) * CH, :] = (
            weight_ref[TAPS * a : TAPS * (a + 1)].reshape(TAPS * CH, CH).T
        )
    rotate(BRK - 1)
    copy.wait()

    def product(i, half, first, second):
        lanes = slice(2 * half * LANES, 2 * (half + 1) * LANES)
        ybuf[i % 2, :, lanes] = jnp.dot(
            wide[...], side_by_side(first, second), preferred_element_type=F32
        )

    def finish(i, half):
        y = ybuf.at[i % 2]
        for j in (2 * half, 2 * half + 1):
            to_high = y[2 * CH :, columns(j)]
            if j > 0:
                to_high = to_high + y[:CH, columns(j - 1)]
            to_low = y[:CH, columns(j)]
            if j < 3:
                to_low = to_low + y[2 * CH :, columns(j + 1)]
            moved = pltpu.roll(jnp.where(low, to_low, to_high), 64, 1)
            total = y[CH : 2 * CH, columns(j)] + features_ref[i, :, columns(j)].astype(F32)
            total = occ_ref[i : i + 1, columns(j)].astype(F32) * ((total + shift) + moved)
            if j in (0, 3):
                edge_ref[i, :, columns(j // 3)] = total
            else:
                middle_ref[i, :, columns(j - 1)] = total.astype(BF)

    for i in range(BRK):
        slots = {
            (dy, dz): i if (dy, dz) == (0, 0) else slot(nb, i, 0, dy, dz)
            for dy in (-1, 0, 1)
            for dz in (-1, 0, 1)
        }
        pieces = []
        for j in range(4):
            pieces.append(
                rotated(
                    merged(lambda kind, dy, dz: acts[kind, slots[dy, dz], :, columns(j)], masks)
                )
            )
            if j % 2 == 1:
                product(i, j // 2, *pieces[-2:])
            if i > 0 and j == 0:
                finish(i - 1, 0)
            if i > 0 and j == 2:
                finish(i - 1, 1)
    finish(BRK - 1, 0)
    finish(BRK - 1, 1)


def sorted_voxels(rows, sort_ref, picked, low):
    sorted_ = [
        jnp.dot(
            jnp.concatenate([rows[k], rows[2 + k]], axis=0),
            sort_ref[k],
            preferred_element_type=F32,
        ).astype(BF)
        for k in range(2)
    ]
    for pair in range(2):
        part = slice(pair * CH, (pair + 1) * CH)
        for j in range(4):
            one, two = sorted_[0][part, columns(j)], sorted_[1][part, columns(j)]
            taps = slice(j * CH, (j + 1) * CH)
            picked[0, taps, columns(pair)] = jnp.where(low, one, two)
            picked[1, taps, columns(pair)] = jnp.where(low, two, one)


def octants(wide2, picked, bias):
    even, odd = (jnp.dot(wide2[c], picked[c], preferred_element_type=F32) for c in range(2))
    both = [
        even[:, columns(pair)] + pltpu.roll(odd[:, columns(pair)], 64, 1) for pair in range(2)
    ]
    return (jnp.concatenate(both, axis=1) + bias).astype(BF)


def outer_kernel(
    nb_ref, map_ref, edge_ref, middle_ref, chip_ref, far_ref, occ_ref, wide, stride_ref, bias_ref,
    sort_ref, entry_ref, place_ref,
    ends_ref, rows_ref, placing_ref, wide2, leave_ref,
    halo, picked, mask, faces, leaving_ends, nb, map_, order, sems,
):
    copies = [
        pltpu.make_async_copy(nb_ref, nb, sems.at[0]),
        pltpu.make_async_copy(map_ref, map_, sems.at[1]),
    ]
    for copy in copies:
        copy.start()
    groups = lax.axis_size("grp")
    device = lax.axis_index("bricks") * groups + lax.axis_index("grp")
    odd = lax.rem(device, 2)
    masks = lane_masks()
    low = masks[2]
    low32 = lax.broadcasted_iota(jnp.int32, (CH, LANES), 1) < 64
    for i in range(BRK):
        halo[odd, i] = chip_ref[i]
        halo[1 - odd, i] = far_ref[i]
        row = slice(i, i + 1)
        mask[i] = jnp.where(
            low32[:1], occ_ref[row, columns(0)], occ_ref[row, columns(3)]
        ).astype(F32)
    halo[0, BRK] = jnp.zeros((CH, LANES), BF)
    halo[1, BRK] = jnp.zeros((CH, LANES), BF)
    for c in range(2):
        taps = jnp.concatenate([stride_ref[2 * k + c] for k in range(4)], axis=0)
        wide2[c] = taps.T
    bias = column(bias_ref[...])
    for copy in copies:
        copy.wait()
    leaving, staying = jnp.int32(0), jnp.int32(HALF)
    for i in range(BRK):
        stays = (map_[0, i] >> 3) == device
        order[jnp.where(stays, staying, leaving)] = i
        staying = staying + stays.astype(jnp.int32)
        leaving = leaving + 1 - stays.astype(jnp.int32)
    brick = [order[k] for k in range(BRK)]

    def raw_of(i):
        def raw(dy, dz):
            return jnp.where(
                low,
                halo[0, slot(nb, i, 1, dy, dz)],
                halo[1, slot(nb, i, -1, dy, dz)],
            )

        return raw

    def product(half, pieces):
        lanes = slice(HALF * half * LANES, HALF * (half + 1) * LANES)
        ends = jnp.concatenate([wide[:CH], wide[2 * CH :]], axis=0)
        faces[:, lanes] = jnp.dot(ends, side_by_side(*pieces), preferred_element_type=F32)

    def finish(k):
        i = brick[k]
        mine = faces[:, columns(k)]
        moved = pltpu.roll(jnp.where(low32, mine[CH:], mine[:CH]), 64, 1) * mask[i]
        for side in range(2):
            keep = low32 if side == 0 else jnp.logical_not(low32)
            fine = (edge_ref[i, :, columns(side)] + jnp.where(keep, moved, 0.0)).astype(BF)
            ends_ref[i, :, columns(side)] = fine
            if k < HALF:
                leaving_ends[k, :, columns(side)] = fine
            else:
                rows_ref[k - HALF, :, columns(2 + side)] = fine
        if k >= HALF:
            rows_ref[k - HALF, :, : 2 * LANES] = middle_ref[i]

    def place(k):
        return entry_ref[...] * place_ref[map_[0, brick[k]] & 7].astype(BF)

    for k in range(HALF):
        placing_ref[k * CH : (k + 1) * CH, :] = place(HALF + k)
    before, result, pieces = None, None, []
    for k in range(BRK + 1):
        now = merged(halo_take(raw_of(brick[k])), masks) if k < BRK else None
        if before is not None:
            spot = k - 1
            pieces.append(rotated(before))
            if spot == 4:
                for q in range(HALF):
                    finish(q)
            if spot % HALF == HALF - 1:
                product(spot // HALF, pieces[-HALF:])
            if spot == 5:
                rows = [
                    jnp.concatenate([middle_ref[brick[q]], leaving_ends[q]], axis=1)
                    for q in range(HALF)
                ]
                sorted_voxels(rows, sort_ref, picked, low)
            if spot == 6:
                result = octants(wide2, picked, bias)
            if spot == 7:
                leave_ref[...] = jnp.dot(
                    result,
                    jnp.concatenate([place(q) for q in range(HALF)], axis=0),
                    preferred_element_type=F32,
                ).astype(BF)
        before = now
    for q in range(HALF, BRK):
        finish(q)


def staying_kernel(
    ends_ref, middle_ref, rows_ref, placing_ref, wide2, sort_ref, bias_ref,
    fine_hbm, stay_ref, picked, sems,
):
    copies = [
        pltpu.make_async_copy(middle_ref, fine_hbm.at[:, :, LANES : 3 * LANES], sems.at[0])
    ] + [
        pltpu.make_async_copy(
            ends_ref.at[:, :, columns(side)], fine_hbm.at[:, :, columns(3 * side)], sems.at[1 + side]
        )
        for side in range(2)
    ]
    for copy in copies:
        copy.start()
    low = lane_masks()[2]
    sorted_voxels([rows_ref[k] for k in range(HALF)], sort_ref, picked, low)
    octant = octants(wide2, picked, column(bias_ref[...]))
    stay_ref[...] = jnp.dot(octant, placing_ref[...], preferred_element_type=F32).astype(BF)
    for copy in copies:
        copy.wait()


def tables():
    voxel = np.arange(VOX)
    x, y, z = voxel >> 6, (voxel >> 3) & 7, voxel & 7
    lane = 64 * (4 * (x & 1) + 2 * (y & 1) + (z & 1)) + 16 * (x >> 1) + 4 * (y >> 1) + (z >> 1)
    sort = np.stack([lane[:, None] == voxel, (lane ^ 64)[:, None] == voxel])
    sort = sort.reshape(2, 4, LANES, VOX)[:, [1, 2, 0, 3]].reshape(2, VOX, VOX)
    sort = sort.astype(ml_dtypes.bfloat16)
    source = 16 * (x & 3) + 4 * (y & 3) + (z & 3)
    entry = (np.arange(64)[:, None] == source[None, :]).astype(ml_dtypes.bfloat16)
    octant = 4 * (x >> 2) + 2 * (y >> 2) + (z >> 2)
    place = (np.arange(8)[:, None, None] == octant).astype(np.float32)
    return sort, entry, place


def shards(
    features,
    occupancy,
    neighbours,
    coarse_map,
    norm_gain,
    time_shift,
    conv_weight,
    stride_weight,
    coarse_bias,
):
    groups = lax.axis_size("grp")
    total = lax.axis_size("bricks") * groups
    vmem = pl.BlockSpec(memory_space=pltpu.VMEM)

    loaded = (
        features,
        occupancy,
        norm_gain.reshape(1, CH),
        time_shift.reshape(1, CH),
        conv_weight,
        neighbours,
        coarse_map.reshape(1, BRK),
        coarse_bias.reshape(1, CH2),
    )
    face, features, occupancy, gain, shift, conv_weight, neighbours, coarse_map, bias = (
        pl.pallas_call(
            faces_kernel,
            in_specs=[pl.BlockSpec(memory_space=pltpu.HBM)] * len(loaded),
            out_specs=[vmem] * (1 + len(loaded)),
            out_shape=[jax.ShapeDtypeStruct((BRK, CH, LANES), BF)]
            + [jax.ShapeDtypeStruct(x.shape, x.dtype) for x in loaded],
            scratch_shapes=[pltpu.SemaphoreType.DMA((len(loaded),))],
            compiler_params=pltpu.CompilerParams(vmem_limit_bytes=8 << 20),
            name="faces",
        )(*(pltpu.with_memory_space_constraint(x, pltpu.HBM) for x in loaded))
    )

    chip = lax.ppermute(face, "grp", [(i, i ^ 1) for i in range(groups)])
    across = [(i, i + 1) for i in range(1, total - 1, 2)]
    far = lax.ppermute(face, ("bricks", "grp"), across + [(j, i) for i, j in across])

    edge, middle, wide = pl.pallas_call(
        inner_kernel,
        in_specs=[vmem] * 6,
        out_specs=[vmem] * 3,
        out_shape=(
            jax.ShapeDtypeStruct((BRK, CH, 2 * LANES), F32),
            jax.ShapeDtypeStruct((BRK, CH, 2 * LANES), BF),
            jax.ShapeDtypeStruct((3 * CH, TAPS * CH), BF),
        ),
        scratch_shapes=[
            pltpu.VMEM((len(ROLLS), BRK + 1, CH, VOX), BF),
            pltpu.VMEM((2, 3 * CH, VOX), F32),
            pltpu.SMEM((BRK, 26), jnp.int32),
            pltpu.SemaphoreType.DMA,
        ],
        compiler_params=pltpu.CompilerParams(vmem_limit_bytes=16 << 20),
        cost_estimate=pl.CostEstimate(
            flops=2 * 27 * CH * CH * VOX * BRK, bytes_accessed=2 << 20, transcendentals=0
        ),
        name="inner",
    )(neighbours, features, occupancy, gain, shift, conv_weight)

    sort, entry, place = (jnp.asarray(table) for table in tables())
    placed = jax.ShapeDtypeStruct((CH2, VOX), BF)
    ends, rows, placing, wide2, leave = pl.pallas_call(
        outer_kernel,
        in_specs=[vmem] * 13,
        out_specs=[vmem] * 5,
        out_shape=(
            jax.ShapeDtypeStruct((BRK, CH, 2 * LANES), BF),
            jax.ShapeDtypeStruct((HALF, CH, VOX), BF),
            jax.ShapeDtypeStruct((HALF * CH, VOX), BF),
            jax.ShapeDtypeStruct((2, CH2, 4 * CH), BF),
            placed,
        ),
        scratch_shapes=[
            pltpu.VMEM((2, BRK + 1, CH, LANES), BF),
            pltpu.VMEM((2, 4 * CH, HALF * CH), BF),
            pltpu.VMEM((BRK, 1, LANES), F32),
            pltpu.VMEM((2 * CH, BRK * LANES), F32),
            pltpu.VMEM((HALF, CH, 2 * LANES), BF),
            pltpu.SMEM((BRK, 26), jnp.int32),
            pltpu.SMEM((1, BRK), jnp.int32),
            pltpu.SMEM((BRK,), jnp.int32),
            pltpu.SemaphoreType.DMA((2,)),
        ],
        compiler_params=pltpu.CompilerParams(vmem_limit_bytes=16 << 20),
        name="outer",
    )(
        neighbours,
        coarse_map,
        edge,
        middle,
        chip,
        far,
        occupancy,
        wide,
        stride_weight,
        bias,
        sort,
        entry,
        place,
    )
    arrived = lax.ppermute(leave, "grp", [(i, i ^ 1) for i in range(groups)])
    fine, stay = pl.pallas_call(
        staying_kernel,
        in_specs=[vmem] * 7,
        out_specs=[pl.BlockSpec(memory_space=pltpu.HBM), vmem],
        out_shape=(jax.ShapeDtypeStruct((BRK, CH, VOX), BF), placed),
        scratch_shapes=[
            pltpu.VMEM((2, 4 * CH, HALF * CH), BF),
            pltpu.SemaphoreType.DMA((3,)),
        ],
        compiler_params=pltpu.CompilerParams(vmem_limit_bytes=8 << 20),
        cost_estimate=pl.CostEstimate(
            flops=2 * 8 * CH * CH2 * VOX * HALF, bytes_accessed=2 << 20, transcendentals=0
        ),
        name="staying",
    )(ends, middle, rows, placing, wide2, sort, bias)
    return fine, (stay + arrived)[None]


def solution(mesh):
    both = ("bricks", "grp")
    return jax.shard_map(
        shards,
        mesh=mesh,
        in_specs=(
            P(both, None, None),
            P(both, None),
            P(both, None),
            P(both),
            P(),
            P(),
            P(),
            P(),
            P(),
        ),
        out_specs=(P(both, None, None), P(both, None, None)),
        check_vma=False,
    )
```

```python
import functools

import jax
import jax.numpy as jnp
import ml_dtypes
import numpy as np
from jax import lax
from jax.experimental import pallas as pl
from jax.experimental.pallas import tpu as pltpu
from jax.sharding import PartitionSpec as P

BF = jnp.bfloat16
F32 = jnp.float32
EPS = 1e-06
BRK = 8
CH = 64
CH2 = 128
VOX = 512
LANES = 128
TAPS = 9

LOADED = 8
HALF = BRK // 2

ROLLS = (0, 64, 8, 120, 72, 56)
PLAIN, SWAP, UP, DOWN, SWAP_UP, SWAP_DOWN = range(6)


def column(row):
    n = row.shape[1]
    wide = jnp.broadcast_to(row, (n, n))
    on = lax.broadcasted_iota(jnp.int32, (n, n), 0) == lax.broadcasted_iota(jnp.int32, (n, n), 1)
    return jnp.sum(jnp.where(on, wide, 0.0), axis=1, keepdims=True)


def scale_of(x):
    return lax.rsqrt(jnp.mean(x * x, axis=0, keepdims=True) + EPS)


def activate(x, scale, occupied, gain):
    normed = x * scale * gain
    return (normed * jax.nn.sigmoid(normed) * occupied).astype(BF)


def position(dx, dy, dz):
    place = 9 * (dx + 1) + 3 * (dy + 1) + (dz + 1)
    return place - 1 if place > 13 else place


def slot(nb_ref, brick, dx, dy, dz):
    target = nb_ref[brick, position(dx, dy, dz)]
    return jnp.where(target < 0, BRK, target & (BRK - 1))


def lane_masks():
    lane = lax.broadcasted_iota(jnp.int32, (CH, LANES), 1)
    z = lane & 7
    y = (lane >> 3) & 7
    return (z == 0, z == 7), {row: y == row for row in (0, 1, 6, 7)}, lane < 64


def merged(take, masks):
    (z0, z7), y, _ = masks
    centre = take(PLAIN, 0, 0)
    up, down = take(UP, 0, 1), take(DOWN, 0, -1)
    above = jnp.where(y[0], take(SWAP, 1, 0), centre)
    below = jnp.where(y[7], take(SWAP, -1, 0), centre)
    return (
        jnp.where(z7, jnp.where(y[6], take(SWAP_DOWN, -1, -1), down), below),
        below,
        jnp.where(z0, jnp.where(y[0], take(SWAP_UP, -1, 1), up), below),
        jnp.where(z7, down, centre),
        centre,
        jnp.where(z0, up, centre),
        jnp.where(z7, jnp.where(y[7], take(SWAP_DOWN, 1, -1), down), above),
        above,
        jnp.where(z0, jnp.where(y[1], take(SWAP_UP, 1, 1), up), above),
    )


def rotated(sources):
    return [
        pltpu.roll(source, turn, 1) if turn else source
        for source, turn in zip(sources, (9, 8, 7, 1, 0, 127, 121, 120, 119))
    ]


def side_by_side(*parts):
    return jnp.concatenate([jnp.concatenate(row, axis=1) for row in zip(*parts)], axis=0)


def halo_take(raw):
    def take(kind, dy, dz):
        piece = raw(dy, dz)
        return pltpu.roll(piece, ROLLS[kind], 1) if ROLLS[kind] else piece

    return take


def columns(j):
    return slice(j * LANES, (j + 1) * LANES)


def faces_kernel(*refs):
    count = LOADED
    sources, face_ref, kept, sems = refs[:count], refs[count], refs[count + 1 : -1], refs[-1]
    copies = [
        pltpu.make_async_copy(source, target, sems.at[k])
        for k, (source, target) in enumerate(zip(sources, kept))
    ]
    for copy in copies:
        copy.start()
    for copy in copies[:3]:
        copy.wait()
    features_ref, occ_ref, gain_ref = kept[:3]
    gain = column(gain_ref[...])
    low = lax.broadcasted_iota(jnp.int32, (CH, LANES), 1) < 64
    for i in range(BRK):
        first, last = features_ref[i, :, columns(0)], features_ref[i, :, columns(3)]
        x = jnp.where(low, first.astype(F32), last.astype(F32))
        row = slice(i, i + 1)
        occupied = jnp.where(low[:1], occ_ref[row, columns(0)], occ_ref[row, columns(3)])
        face_ref[i] = activate(x, scale_of(x), occupied.astype(F32), gain)
    for copy in copies[3:]:
        copy.wait()


def inner_kernel(
    nb_ref, features_ref, occ_ref, gain_ref, shift_ref, weight_ref, edge_ref, middle_ref, wide,
    acts, ybuf, nb, sem,
):
    copy = pltpu.make_async_copy(nb_ref, nb, sem)
    copy.start()
    gain = column(gain_ref[...])
    shift = column(shift_ref[...])
    masks = lane_masks()
    low = lax.broadcasted_iota(jnp.int32, (CH, LANES), 1) < 64
    for kind in range(len(ROLLS)):
        acts[kind, BRK] = jnp.zeros((CH, VOX), BF)

    lane = lax.broadcasted_iota(jnp.int32, (LANES, 2 * LANES), 1)
    turn = jnp.where(lane < LANES, ROLLS[SWAP_UP], ROLLS[SWAP_DOWN])
    origin = lax.broadcasted_iota(jnp.int32, (LANES, 2 * LANES), 0)
    turns = (origin == ((lane - turn) & (LANES - 1))).astype(F32).astype(BF)

    def rotate(i):
        for j in range(4):
            piece = acts[PLAIN, i, :, columns(j)]
            for kind in (SWAP, UP, DOWN):
                acts[kind, i, :, columns(j)] = pltpu.roll(piece, ROLLS[kind], 1)
        rows = jnp.concatenate([acts[PLAIN, i, :, columns(j)] for j in range(4)], axis=0)
        both = jnp.dot(rows, turns, preferred_element_type=F32).astype(BF)
        for j in range(4):
            for k, kind in enumerate((SWAP_UP, SWAP_DOWN)):
                acts[kind, i, :, columns(j)] = both[j * CH : (j + 1) * CH, columns(k)]

    scale = scale_of(features_ref[0].astype(F32))
    for i in range(BRK):
        upcoming = scale_of(features_ref[i + 1].astype(F32)) if i + 1 < BRK else None
        occupied = occ_ref[i : i + 1, :].astype(F32)
        acts[PLAIN, i] = activate(features_ref[i].astype(F32), scale, occupied, gain)
        if i > 0:
            rotate(i - 1)
        scale = upcoming
    for a in range(3):
        wide[a * CH : (a + 1) * CH, :] = (
            weight_ref[TAPS * a : TAPS * (a + 1)].reshape(TAPS * CH, CH).T
        )
    rotate(BRK - 1)
    copy.wait()

    def product(i, half, first, second):
        lanes = slice(2 * half * LANES, 2 * (half + 1) * LANES)
        ybuf[i % 2, :, lanes] = jnp.dot(
            wide[...], side_by_side(first, second), preferred_element_type=F32
        )

    def finish(i, half):
        y = ybuf.at[i % 2]
        for j in (2 * half, 2 * half + 1):
            to_high = y[2 * CH :, columns(j)]
            if j > 0:
                to_high = to_high + y[:CH, columns(j - 1)]
            to_low = y[:CH, columns(j)]
            if j < 3:
                to_low = to_low + y[2 * CH :, columns(j + 1)]
            moved = pltpu.roll(jnp.where(low, to_low, to_high), 64, 1)
            total = y[CH : 2 * CH, columns(j)] + features_ref[i, :, columns(j)].astype(F32)
            total = occ_ref[i : i + 1, columns(j)].astype(F32) * ((total + shift) + moved)
            if j in (0, 3):
                edge_ref[i, :, columns(j // 3)] = total
            else:
                middle_ref[i, :, columns(j - 1)] = total.astype(BF)

    for i in range(BRK):
        slots = {
            (dy, dz): i if (dy, dz) == (0, 0) else slot(nb, i, 0, dy, dz)
            for dy in (-1, 0, 1)
            for dz in (-1, 0, 1)
        }
        pieces = []
        for j in range(4):
            pieces.append(
                rotated(
                    merged(lambda kind, dy, dz: acts[kind, slots[dy, dz], :, columns(j)], masks)
                )
            )
            if j % 2 == 1:
                product(i, j // 2, *pieces[-2:])
            if i > 0 and j == 0:
                finish(i - 1, 0)
            if i > 0 and j == 2:
                finish(i - 1, 1)
    finish(BRK - 1, 0)
    finish(BRK - 1, 1)


def sorted_voxels(rows, sort_ref, picked, low):
    sorted_ = [
        jnp.dot(
            jnp.concatenate([rows[k], rows[2 + k]], axis=0),
            sort_ref[k],
            preferred_element_type=F32,
        ).astype(BF)
        for k in range(2)
    ]
    for pair in range(2):
        part = slice(pair * CH, (pair + 1) * CH)
        for j in range(4):
            one, two = sorted_[0][part, columns(j)], sorted_[1][part, columns(j)]
            taps = slice(j * CH, (j + 1) * CH)
            picked[0, taps, columns(pair)] = jnp.where(low, one, two)
            picked[1, taps, columns(pair)] = jnp.where(low, two, one)


def octants(wide2, picked, bias):
    even, odd = (jnp.dot(wide2[c], picked[c], preferred_element_type=F32) for c in range(2))
    both = [
        even[:, columns(pair)] + pltpu.roll(odd[:, columns(pair)], 64, 1) for pair in range(2)
    ]
    return (jnp.concatenate(both, axis=1) + bias).astype(BF)


def outer_kernel(
    nb_ref, map_ref, edge_ref, middle_ref, chip_ref, far_ref, occ_ref, wide, stride_ref, bias_ref,
    sort_ref, entry_ref, place_ref,
    ends_ref, rows_ref, placing_ref, wide2, leave_ref,
    halo, picked, mask, faces, leaving_ends, nb, map_, order, sems,
):
    copies = [
        pltpu.make_async_copy(nb_ref, nb, sems.at[0]),
        pltpu.make_async_copy(map_ref, map_, sems.at[1]),
    ]
    for copy in copies:
        copy.start()
    groups = lax.axis_size("grp")
    device = lax.axis_index("bricks") * groups + lax.axis_index("grp")
    odd = lax.rem(device, 2)
    masks = lane_masks()
    low = masks[2]
    low32 = lax.broadcasted_iota(jnp.int32, (CH, LANES), 1) < 64
    for i in range(BRK):
        halo[odd, i] = chip_ref[i]
        halo[1 - odd, i] = far_ref[i]
        row = slice(i, i + 1)
        mask[i] = jnp.where(
            low32[:1], occ_ref[row, columns(0)], occ_ref[row, columns(3)]
        ).astype(F32)
    halo[0, BRK] = jnp.zeros((CH, LANES), BF)
    halo[1, BRK] = jnp.zeros((CH, LANES), BF)
    for c in range(2):
        taps = jnp.concatenate([stride_ref[2 * k + c] for k in range(4)], axis=0)
        wide2[c] = taps.T
    bias = column(bias_ref[...])
    for copy in copies:
        copy.wait()
    leaving, staying = jnp.int32(0), jnp.int32(HALF)
    for i in range(BRK):
        stays = (map_[0, i] >> 3) == device
        order[jnp.where(stays, staying, leaving)] = i
        staying = staying + stays.astype(jnp.int32)
        leaving = leaving + 1 - stays.astype(jnp.int32)
    brick = [order[k] for k in range(BRK)]

    def raw_of(i):
        def raw(dy, dz):
            return jnp.where(
                low,
                halo[0, slot(nb, i, 1, dy, dz)],
                halo[1, slot(nb, i, -1, dy, dz)],
            )

        return raw

    def product(half, pieces):
        lanes = slice(HALF * half * LANES, HALF * (half + 1) * LANES)
        ends = jnp.concatenate([wide[:CH], wide[2 * CH :]], axis=0)
        faces[:, lanes] = jnp.dot(ends, side_by_side(*pieces), preferred_element_type=F32)

    def finish(k):
        i = brick[k]
        mine = faces[:, columns(k)]
        moved = pltpu.roll(jnp.where(low32, mine[CH:], mine[:CH]), 64, 1) * mask[i]
        for side in range(2):
            keep = low32 if side == 0 else jnp.logical_not(low32)
            fine = (edge_ref[i, :, columns(side)] + jnp.where(keep, moved, 0.0)).astype(BF)
            ends_ref[i, :, columns(side)] = fine
            if k < HALF:
                leaving_ends[k, :, columns(side)] = fine
            else:
                rows_ref[k - HALF, :, columns(2 + side)] = fine
        if k >= HALF:
            rows_ref[k - HALF, :, : 2 * LANES] = middle_ref[i]

    def place(k):
        return entry_ref[...] * place_ref[map_[0, brick[k]] & 7].astype(BF)

    before, result, pieces = None, None, []
    for k in range(BRK + 1):
        now = merged(halo_take(raw_of(brick[k])), masks) if k < BRK else None
        if before is not None:
            spot = k - 1
            pieces.append(rotated(before))
            if spot == 4:
                for q in range(HALF):
                    finish(q)
            if spot % HALF == HALF - 1:
                product(spot // HALF, pieces[-HALF:])
            if spot == 5:
                rows = [
                    jnp.concatenate([middle_ref[brick[q]], leaving_ends[q]], axis=1)
                    for q in range(HALF)
                ]
                sorted_voxels(rows, sort_ref, picked, low)
            if spot == 6:
                result = octants(wide2, picked, bias)
            if spot == 7:
                leave_ref[...] = jnp.dot(
                    result,
                    jnp.concatenate([place(q) for q in range(HALF)], axis=0),
                    preferred_element_type=F32,
                ).astype(BF)
        before = now
    for k in range(HALF):
        placing_ref[k * CH : (k + 1) * CH, :] = place(HALF + k)
    for q in range(HALF, BRK):
        finish(q)


def staying_kernel(
    ends_ref, middle_ref, rows_ref, placing_ref, wide2, sort_ref, bias_ref,
    fine_hbm, stay_ref, picked, sems,
):
    copies = [
        pltpu.make_async_copy(middle_ref, fine_hbm.at[:, :, LANES : 3 * LANES], sems.at[0])
    ] + [
        pltpu.make_async_copy(
            ends_ref.at[:, :, columns(side)], fine_hbm.at[:, :, columns(3 * side)], sems.at[1 + side]
        )
        for side in range(2)
    ]
    for copy in copies:
        copy.start()
    low = lane_masks()[2]
    sorted_voxels([rows_ref[k] for k in range(HALF)], sort_ref, picked, low)
    octant = octants(wide2, picked, column(bias_ref[...]))
    stay_ref[...] = jnp.dot(octant, placing_ref[...], preferred_element_type=F32).astype(BF)
    for copy in copies:
        copy.wait()


def tables():
    voxel = np.arange(VOX)
    x, y, z = voxel >> 6, (voxel >> 3) & 7, voxel & 7
    lane = 64 * (4 * (x & 1) + 2 * (y & 1) + (z & 1)) + 16 * (x >> 1) + 4 * (y >> 1) + (z >> 1)
    sort = np.stack([lane[:, None] == voxel, (lane ^ 64)[:, None] == voxel])
    sort = sort.reshape(2, 4, LANES, VOX)[:, [1, 2, 0, 3]].reshape(2, VOX, VOX)
    sort = sort.astype(ml_dtypes.bfloat16)
    source = 16 * (x & 3) + 4 * (y & 3) + (z & 3)
    entry = (np.arange(64)[:, None] == source[None, :]).astype(ml_dtypes.bfloat16)
    octant = 4 * (x >> 2) + 2 * (y >> 2) + (z >> 2)
    place = (np.arange(8)[:, None, None] == octant).astype(np.float32)
    return sort, entry, place


def shards(
    features,
    occupancy,
    neighbours,
    coarse_map,
    norm_gain,
    time_shift,
    conv_weight,
    stride_weight,
    coarse_bias,
):
    groups = lax.axis_size("grp")
    total = lax.axis_size("bricks") * groups
    vmem = pl.BlockSpec(memory_space=pltpu.VMEM)

    loaded = (
        features,
        occupancy,
        norm_gain.reshape(1, CH),
        time_shift.reshape(1, CH),
        conv_weight,
        neighbours,
        coarse_map.reshape(1, BRK),
        coarse_bias.reshape(1, CH2),
    )
    face, features, occupancy, gain, shift, conv_weight, neighbours, coarse_map, bias = (
        pl.pallas_call(
            faces_kernel,
            in_specs=[pl.BlockSpec(memory_space=pltpu.HBM)] * len(loaded),
            out_specs=[vmem] * (1 + len(loaded)),
            out_shape=[jax.ShapeDtypeStruct((BRK, CH, LANES), BF)]
            + [jax.ShapeDtypeStruct(x.shape, x.dtype) for x in loaded],
            scratch_shapes=[pltpu.SemaphoreType.DMA((len(loaded),))],
            compiler_params=pltpu.CompilerParams(vmem_limit_bytes=8 << 20),
            name="faces",
        )(*(pltpu.with_memory_space_constraint(x, pltpu.HBM) for x in loaded))
    )

    chip = lax.ppermute(face, "grp", [(i, i ^ 1) for i in range(groups)])
    across = [(i, i + 1) for i in range(1, total - 1, 2)]
    far = lax.ppermute(face, ("bricks", "grp"), across + [(j, i) for i, j in across])

    edge, middle, wide = pl.pallas_call(
        inner_kernel,
        in_specs=[vmem] * 6,
        out_specs=[vmem] * 3,
        out_shape=(
            jax.ShapeDtypeStruct((BRK, CH, 2 * LANES), F32),
            jax.ShapeDtypeStruct((BRK, CH, 2 * LANES), BF),
            jax.ShapeDtypeStruct((3 * CH, TAPS * CH), BF),
        ),
        scratch_shapes=[
            pltpu.VMEM((len(ROLLS), BRK + 1, CH, VOX), BF),
            pltpu.VMEM((2, 3 * CH, VOX), F32),
            pltpu.SMEM((BRK, 26), jnp.int32),
            pltpu.SemaphoreType.DMA,
        ],
        compiler_params=pltpu.CompilerParams(vmem_limit_bytes=16 << 20),
        cost_estimate=pl.CostEstimate(
            flops=2 * 27 * CH * CH * VOX * BRK, bytes_accessed=2 << 20, transcendentals=0
        ),
        name="inner",
    )(neighbours, features, occupancy, gain, shift, conv_weight)

    sort, entry, place = (jnp.asarray(table) for table in tables())
    placed = jax.ShapeDtypeStruct((CH2, VOX), BF)
    ends, rows, placing, wide2, leave = pl.pallas_call(
        outer_kernel,
        in_specs=[vmem] * 13,
        out_specs=[vmem] * 5,
        out_shape=(
            jax.ShapeDtypeStruct((BRK, CH, 2 * LANES), BF),
            jax.ShapeDtypeStruct((HALF, CH, VOX), BF),
            jax.ShapeDtypeStruct((HALF * CH, VOX), BF),
            jax.ShapeDtypeStruct((2, CH2, 4 * CH), BF),
            placed,
        ),
        scratch_shapes=[
            pltpu.VMEM((2, BRK + 1, CH, LANES), BF),
            pltpu.VMEM((2, 4 * CH, HALF * CH), BF),
            pltpu.VMEM((BRK, 1, LANES), F32),
            pltpu.VMEM((2 * CH, BRK * LANES), F32),
            pltpu.VMEM((HALF, CH, 2 * LANES), BF),
            pltpu.SMEM((BRK, 26), jnp.int32),
            pltpu.SMEM((1, BRK), jnp.int32),
            pltpu.SMEM((BRK,), jnp.int32),
            pltpu.SemaphoreType.DMA((2,)),
        ],
        compiler_params=pltpu.CompilerParams(vmem_limit_bytes=16 << 20),
        name="outer",
    )(
        neighbours,
        coarse_map,
        edge,
        middle,
        chip,
        far,
        occupancy,
        wide,
        stride_weight,
        bias,
        sort,
        entry,
        place,
    )
    arrived = lax.ppermute(leave, "grp", [(i, i ^ 1) for i in range(groups)])
    fine, stay = pl.pallas_call(
        staying_kernel,
        in_specs=[vmem] * 7,
        out_specs=[pl.BlockSpec(memory_space=pltpu.HBM), vmem],
        out_shape=(jax.ShapeDtypeStruct((BRK, CH, VOX), BF), placed),
        scratch_shapes=[
            pltpu.VMEM((2, 4 * CH, HALF * CH), BF),
            pltpu.SemaphoreType.DMA((3,)),
        ],
        compiler_params=pltpu.CompilerParams(vmem_limit_bytes=8 << 20),
        cost_estimate=pl.CostEstimate(
            flops=2 * 8 * CH * CH2 * VOX * HALF, bytes_accessed=2 << 20, transcendentals=0
        ),
        name="staying",
    )(ends, middle, rows, placing, wide2, sort, bias)
    return fine, (stay + arrived)[None]


def solution(mesh):
    both = ("bricks", "grp")
    return jax.shard_map(
        shards,
        mesh=mesh,
        in_specs=(
            P(both, None, None),
            P(both, None),
            P(both, None),
            P(both),
            P(),
            P(),
            P(),
            P(),
            P(),
        ),
        out_specs=(P(both, None, None), P(both, None, None)),
        check_vma=False,
    )
```
